32 devices in a mesh: arc: 16 (over z, x, core), ord: 2 (over y).
Axes of the slice: x: 2, y: 2, z: 4, core: 2. Of those that a mesh axis runs over, the one named last changes fastest.
Arguments:
- design: bfloat16 [16384, 32768], P('arc', 'ord'), may hold values from -4 to 4
- arc_lengths: int32 [16], P('arc'), may hold values from 1 to 1024, 10240 in all
- kaula_prior: float32 [1024], replicated, may hold values from 1 to 20
Outputs:
- factor: float32 [1024, 32768], P('arc', 'ord')
The draws below stay inside these ranges and needn't reach their ends.
Inputs may be any that keep to these rules, and one draw needn't show every extreme that they name: `arc_lengths`: some arc has all 1024 slots live.
All inputs are finite; a program needn't handle non-finite values. No bound on the sum of `arc_lengths` on one device may be relied on, other than what follows from the above.
Results may differ from the reference program's by a relative error of at most 0.0003.
Values may be sent and summed in bfloat16 or wider, within the bound.
A program may use at most 320 MiB of HBM per device.

```python
import math
import jax
import jax.numpy as jnp
import numpy as np
from jax import lax

TILE = 512
PANELS = 2
COEFFS = 32768
STEPS = 1024
SLAB = 1024
ARCS = 16
OBSERVATIONS = 16384


def draw_design(key, part):
    taps = 8
    wide = COEFFS + taps - 1
    scale_back = 1.0 / math.sqrt(12.0)

    def one_block(index):
        sub = jax.random.fold_in(key, index)
        first_key, second_key = jax.random.split(sub)
        source = jax.random.normal(first_key, (STEPS, wide), jnp.float32)
        white = jax.random.normal(second_key, (STEPS, COEFFS), jnp.float32)
        total = source[:, 0:COEFFS]
        for shift in range(1, taps):
            total = total + source[:, shift:shift + COEFFS]
        total = total + 2.0 * white
        return jnp.clip(total * scale_back, -4.0, 4.0).astype(jnp.bfloat16)
    blocks = lax.map(one_block, jnp.arange(ARCS, dtype=jnp.int32))
    return blocks.reshape(OBSERVATIONS, COEFFS)


def length_profile(amount, total, limit, slope):
    loads = [(1 << 20) // math.isqrt(grade ** slope) + 1 for grade in range(2, amount + 1)]
    surplus, holding = total - limit - (amount - 1), [1] * (amount - 1)
    while surplus > 0:
        free = [i for i in range(amount - 1) if holding[i] < limit]
        pool, left = sum([loads[i] for i in free]), surplus
        for i in free:
            more = min(limit - holding[i], max(1, left * loads[i] // pool), surplus)
            holding[i] = holding[i] + more
            surplus = surplus - more
    return np.array([limit] + holding)


def uneven(key, amount, total, bound, lean):
    if amount == 2:
        one = jax.random.randint(key, (), max(1, total - bound), min(bound, total - 1) + 1)
        return jnp.stack([one, total - one])
    sizes = jnp.asarray(length_profile(amount, total, bound, lean), jnp.int32)
    twos = (amount - 1) // 2
    giver, receiver = sizes[1:1 + 2 * twos:2], sizes[2:2 + 2 * twos:2]
    room = jnp.minimum(giver - 1, bound - receiver)
    passed = jax.random.randint(jax.random.fold_in(key, 1), (twos,), 0, 1 << 20) % (room + 1)
    sizes = sizes.at[1:1 + 2 * twos:2].set(giver - passed).at[2:2 + 2 * twos:2].set(receiver + passed)
    return sizes[jax.random.permutation(jax.random.fold_in(key, 2), amount)]


def setup_inputs(seed: int = 0) -> dict:
    key_of = jax.random.split(jax.random.key(seed), 4)
    design = draw_design(jax.random.fold_in(key_of[3], 71), 0)
    arc_lengths = uneven(key_of[1], ARCS, ARCS * STEPS * 5 // 8, STEPS, 2).astype(jnp.int32)
    kaula_prior = jnp.clip(jnp.exp(jax.random.uniform(key_of[2], (SLAB,), jnp.float32, math.log(1.0), math.log(20.0))), 1.0, 20.0)
    return dict(design=design, arc_lengths=arc_lengths, kaula_prior=kaula_prior)


def reference(design, arc_lengths, kaula_prior):
    total_rows = design.shape[0]
    row_ids = jnp.arange(total_rows, dtype=jnp.int32)
    arc_of = (row_ids // STEPS).astype(jnp.int32)
    in_arc = row_ids % STEPS
    is_live = in_arc < arc_lengths[arc_of]
    masked = jnp.where(is_live[:, None], design[:, :SLAB], jnp.zeros((), design.dtype))
    normal = jnp.dot(masked.T.astype(jnp.float32), design.astype(jnp.float32), preferred_element_type=jnp.float32) * (1.0 / math.sqrt(OBSERVATIONS))
    diag_ids = jnp.arange(SLAB, dtype=jnp.int32)
    normal = normal.at[diag_ids, diag_ids].add(kaula_prior)
    blocks = [normal[p * TILE:(p + 1) * TILE] for p in range(PANELS)]
    for p in range(PANELS):
        lower_factor = jnp.linalg.cholesky(blocks[p][:, p * TILE:(p + 1) * TILE])
        blocks[p] = jax.scipy.linalg.solve_triangular(lower_factor, blocks[p], lower=True)
        for q in range(p + 1, PANELS):
            upper_tile = blocks[p][:, q * TILE:(q + 1) * TILE]
            blocks[q] = blocks[q] - jnp.dot(upper_tile.T, blocks[p], precision=lax.Precision.HIGHEST)
    return jnp.concatenate(blocks, axis=0)
```

```python
import functools
import math

import jax
import jax.numpy as jnp
from jax import lax
from jax.experimental import pallas as pl
from jax.experimental.pallas import tpu as pltpu
from jax.sharding import PartitionSpec as P

TILE = 512
PANELS = 2


def broadcast(block, axis, source):
    block = jnp.where(lax.axis_index(axis) == source, block, jnp.zeros_like(block))
    return lax.psum(block, axis)


def apply_panels(matrix, lowers, couplings):
    blocks = [matrix[p * TILE : (p + 1) * TILE] for p in range(PANELS)]
    for p in range(PANELS):
        blocks[p] = jax.scipy.linalg.solve_triangular(lowers[p], blocks[p], lower=True)
        for q in range(p + 1, PANELS):
            blocks[q] = blocks[q] - jnp.dot(
                couplings[p, q].T, blocks[p], precision=lax.Precision.HIGHEST
            )
    return jnp.concatenate(blocks, axis=0)


def on_device(design, arc_lengths, kaula_prior):
    obs_dev, ord_cols = design.shape
    arcs_here = arc_lengths.shape[0]
    arc_steps = obs_dev // arcs_here
    row_block = min(256, arc_steps)
    slab_rows = TILE * PANELS
    pieces = []
    for panel_index in range(PANELS):
        owner = panel_index * TILE // ord_cols
        offset = panel_index * TILE % ord_cols
        piece = design[:, offset : offset + TILE]
        pieces.append(broadcast(piece, "ord", owner))
    slab_cols = jnp.concatenate(pieces, axis=1)
    position = lax.broadcasted_iota(jnp.int32, (row_block, 1), 0)
    partial_value = jnp.zeros((slab_rows, ord_cols), jnp.float32)
    gram_part = jnp.zeros((slab_rows, slab_rows), jnp.float32)
    arc_slot = 0
    length = arc_lengths[arc_slot]
    blocks_live = (length + row_block - 1) // row_block

    def accumulate(step_idx, running, arc_slot=arc_slot, length=length):
        first_row = arc_slot * arc_steps + step_idx * row_block
        slab_block = lax.dynamic_slice_in_dim(slab_cols, first_row, row_block, 0)
        tile_block = lax.dynamic_slice_in_dim(design, first_row, row_block, 0)
        is_live = position + step_idx * row_block < length
        live_block = jnp.where(is_live, slab_block, jnp.zeros((), slab_block.dtype))
        dims = (((0,), (0,)), ((), ()))
        normal_acc = running[0] + lax.dot_general(
            live_block, tile_block, dims, preferred_element_type=jnp.float32
        )
        gram_acc = running[1] + lax.dot_general(
            live_block, slab_block, dims, preferred_element_type=jnp.float32
        )
        return (normal_acc, gram_acc)

    partial_value, gram_part = lax.fori_loop(0, blocks_live, accumulate, (partial_value, gram_part))
    inverse_norm = 1.0 / math.sqrt(lax.axis_size("arc") * obs_dev)
    square_ids = lax.broadcasted_iota(jnp.int32, (slab_rows, slab_rows), 0)
    square_cols = lax.broadcasted_iota(jnp.int32, (slab_rows, slab_rows), 1)
    gram = lax.psum(gram_part, "arc") * inverse_norm
    gram = gram + jnp.where(square_ids == square_cols, kaula_prior[:, None], 0.0)
    gram_blocks = [gram[p * TILE : (p + 1) * TILE] for p in range(PANELS)]
    lowers = []
    couplings = {}
    for p in range(PANELS):
        lower_factor = jnp.linalg.cholesky(gram_blocks[p][:, p * TILE : (p + 1) * TILE])
        lowers.append(lower_factor)
        gram_blocks[p] = jax.scipy.linalg.solve_triangular(lower_factor, gram_blocks[p], lower=True)
        for q in range(p + 1, PANELS):
            upper_tile = gram_blocks[p][:, q * TILE : (q + 1) * TILE]
            couplings[p, q] = upper_tile
            gram_blocks[q] = gram_blocks[q] - jnp.dot(
                upper_tile.T, gram_blocks[p], precision=lax.Precision.HIGHEST
            )
    row_index = lax.broadcasted_iota(jnp.int32, (slab_rows, 1), 0)
    summed = lax.psum_scatter(partial_value, "arc", scatter_dimension=1, tiled=True) * inverse_norm
    width = ord_cols // lax.axis_size("arc")
    col_first = lax.axis_index("ord") * ord_cols + lax.axis_index("arc") * width
    global_col = col_first + lax.broadcasted_iota(jnp.int32, (1, width), 1)
    matrix = summed + jnp.where(row_index == global_col, kaula_prior[:, None], 0.0)
    share = apply_panels(matrix, lowers, couplings)
    factor = lax.all_to_all(share, "arc", split_axis=0, concat_axis=1, tiled=True)
    return factor


NB = 128
BAND = 5
GROUP = 64
LEVELS = 32760.0
PAD = 16
COLS = 256
VMEM_BYTES = 48 << 20
F32 = jnp.float32
BF16 = jnp.bfloat16


def params():
    return pltpu.CompilerParams(vmem_limit_bytes=VMEM_BYTES)


def cost(flops, moved):
    return pl.CostEstimate(flops=flops, bytes_accessed=moved, transcendentals=0)


def tree_sum(terms):
    while len(terms) > 1:
        pairs = [terms[i] + terms[i + 1] for i in range(0, len(terms) - 1, 2)]
        terms = pairs + ([terms[-1]] if len(terms) % 2 else [])
    return terms[0]


def diagonal_inverse(block):
    tiles = NB // 8
    sub = lax.broadcasted_iota(jnp.int32, (8, NB), 0)
    lane = lax.broadcasted_iota(jnp.int32, (8, NB), 1)
    rest = [block[8 * t : 8 * t + 8] for t in range(tiles)]
    inv = [jnp.where(sub + 8 * t == lane, 1.0, 0.0).astype(F32) for t in range(tiles)]

    def lanes(value, j):
        return jnp.broadcast_to(value[:, j : j + 1], (8, NB))

    def rows(value):
        return [jnp.broadcast_to(value[s : s + 1], (8, NB)) for s in range(8)]

    def combine(columns, row_values):
        return tree_sum([c * r for c, r in zip(columns, row_values)])

    for t in range(tiles):
        column = [lanes(rest[t], 8 * t + s) for s in range(8)]
        unit = [jnp.where(sub == s, 1.0, 0.0).astype(F32) for s in range(8)]
        whole = list(unit)
        pivots = jnp.ones((8, NB), F32)
        for s in range(8):
            pivot = jnp.broadcast_to(column[s][s : s + 1], (8, NB))
            recip = 1.0 / pivot
            pivots = jnp.where(sub == s, pivot, pivots)
            scaled = column[s] * recip
            below = jnp.where(sub > s, scaled, 0.0)
            others = jnp.where(sub == s, 1.0 - recip, scaled)
            for q in range(s + 1, 8):
                column[q] = column[q] - others * jnp.broadcast_to(column[q][s : s + 1], (8, NB))
            for q in range(s + 1):
                whole[q] = whole[q] - others * jnp.broadcast_to(whole[q][s : s + 1], (8, NB))
                unit[q] = unit[q] - below * jnp.broadcast_to(unit[q][s : s + 1], (8, NB))
        inv_rows = rows(inv[t])
        if t + 1 < tiles:
            solved = rows(combine(whole, rows(rest[t])))
            inv_solved = rows(combine(whole, inv_rows))
            for i in range(t + 1, tiles):
                columns = [lanes(rest[i], 8 * t + s) for s in range(8)]
                rest[i] = rest[i] - combine(columns, solved)
                inv[i] = inv[i] - combine(columns, inv_solved)
        inv[t] = combine(unit, inv_rows) * (1.0 / jnp.sqrt(pivots))
    return jnp.concatenate(inv, axis=0)


def exact_dot(a, b):
    return jnp.dot(a, b, precision=lax.Precision.HIGHEST)


def factor_kernel(scale, band_ref, prior_ref, work, upper, left):
    size = work.shape[0]
    blocks = size // NB
    sub = lax.broadcasted_iota(jnp.int32, (NB, NB), 0)
    lane = lax.broadcasted_iota(jnp.int32, (NB, NB), 1)
    eye = jnp.where(sub == lane, 1.0, 0.0).astype(F32)
    zero = jnp.zeros((NB, NB), F32)
    for i in range(blocks):
        here = slice(i * NB, (i + 1) * NB)
        for j in range(blocks):
            there = slice(j * NB, (j + 1) * NB)
            if j < i:
                value = zero
            elif j - i < BAND:
                value = band_ref[here, (j - i) * NB : (j - i + 1) * NB] * scale
            else:
                d = i - j + blocks
                value = band_ref[there, d * NB : (d + 1) * NB].T * scale
            if i == j:
                value = value + eye * prior_ref[i : i + 1, :]
            work[here, there] = value

    def step(k, carry):
        here = pl.ds(pl.multiple_of(k * NB, NB), NB)
        block = work[here, here]
        inverse = diagonal_inverse(block)
        work[here, here] = eye
        left[...] = exact_dot(inverse, work[here, :])
        work[here, :] = left[...]
        column = lax.broadcasted_iota(jnp.int32, (NB, size), 1)
        upper[here, :] = jnp.where(column >= (k + 1) * NB, left[...], 0.0)
        upper[here, here] = exact_dot(inverse, block)

        def update(i, carry):
            there = pl.ds(pl.multiple_of(i * NB, NB), NB)
            work[there, here] = zero
            work[there, :] -= exact_dot(left[:, there].T, left[...])
            return carry

        return lax.fori_loop(k + 1, blocks, update, carry)

    lax.fori_loop(0, blocks, step, 0)
    for k in range(blocks - 1):
        work[k * NB : (k + 1) * NB, (k + 1) * NB :] = jnp.zeros((NB, size - (k + 1) * NB), F32)


def factorize(band, prior, scale):
    size = band.shape[0]
    square = jax.ShapeDtypeStruct((size, size), F32)
    vmem = pl.BlockSpec(memory_space=pltpu.VMEM)
    return pl.pallas_call(
        functools.partial(factor_kernel, scale),
        out_shape=(square, square),
        in_specs=[vmem, vmem],
        out_specs=(vmem, vmem),
        scratch_shapes=[pltpu.VMEM((NB, size), F32)],
        compiler_params=params(),
        cost_estimate=cost(70_000_000_000, 12 << 20),
    )(band, prior.reshape(size // NB, NB))


MESH = pl.DeviceIdType.MESH


def opening_kernel(
    length_ref, design_ref, own_ref, other_ref, raw_ref, band_ref,
    slab, mask, band, sums, first, second, third, fourth, last,
    local_sem, raw_send, raw_recv, mask_send, mask_recv, swap_send, swap_recv, hop_send, hop_recv,
):
    steps, ord_cols = design_ref.shape
    size = slab.shape[1]
    blocks = size // NB
    half, quarter = size // 2, ord_cols // 8
    me, order = lax.axis_index("arc"), lax.axis_index("ord")
    core, x, low, high = me % 2, me // 2 % 2, me // 4 % 2, me // 8
    peer = [
        (me + 1 - 2 * core, order),
        (me + 2 - 4 * x, order),
        (me + 4 - 8 * low, order),
        (me + 8 - 16 * high, order),
    ]
    across = (me, 1 - order)

    barrier = pltpu.get_barrier_semaphore()
    for device in peer + [across]:
        pl.semaphore_signal(barrier, inc=1, device_id=device, device_id_type=MESH)
    pl.semaphore_wait(barrier, 5)

    def remote(source, target, send_sem, recv_sem, device):
        return pltpu.make_async_remote_copy(
            src_ref=source, dst_ref=target, send_sem=send_sem, recv_sem=recv_sem,
            device_id=device, device_id_type=MESH,
        )

    raws = []
    for k in range(4):
        z = 2 * (high if k < 2 else 1 - high) + (low if k % 2 == 0 else 1 - low)
        columns = pl.ds(pl.multiple_of((1 - core) * 4 * quarter + z * quarter, quarter), quarter)
        raws.append(
            remote(design_ref.at[:, columns], raw_ref.at[k], raw_send.at[k], raw_recv.at[k], peer[0])
        )
    masks = [
        remote(mask.at[h], mask.at[h], mask_send.at[h], mask_recv.at[h], across) for h in range(2)
    ]
    swaps = [
        remote(mask.at[h], other_ref.at[h], swap_send.at[h], swap_recv.at[h], peer[0]) for h in range(2)
    ]
    keeps = [pltpu.make_async_copy(mask.at[h], own_ref.at[h], local_sem.at[1 + h]) for h in range(2)]
    hops = [
        remote(band.at[:, :, :, 1 - core], first, hop_send.at[0], hop_recv.at[0], peer[0]),
        remote(sums.at[:, :, 1 - x], second, hop_send.at[1], hop_recv.at[1], peer[1]),
        remote(second.at[:, 1 - low], third, hop_send.at[2], hop_recv.at[2], peer[2]),
        remote(third.at[1 - high], fourth, hop_send.at[3], hop_recv.at[3], peer[3]),
        remote(fourth, last, hop_send.at[4], hop_recv.at[4], across),
    ]

    @pl.when(order == 0)
    def _():
        load = pltpu.make_async_copy(design_ref.at[:, pl.ds(0, size)], slab, local_sem.at[0])
        load.start()
        load.wait()
        position = lax.broadcasted_iota(jnp.int32, (steps, NB), 0)
        per = blocks // 2
        for h in range(2):
            for i in range(per):
                piece = slab[:, (h * per + i) * NB : (h * per + i + 1) * NB].astype(F32)
                piece = jnp.where(position < length_ref[0], piece, 0.0)
                mask[h, i * NB : (i + 1) * NB, :] = piece.T.astype(BF16)
            masks[h].start()
            swaps[h].start()
            keeps[h].start()
        for raw in raws:
            raw.start()
        for i in range(blocks):
            rows = mask[i // per, i % per * NB : (i % per + 1) * NB, :]
            for d in range(BAND):
                j = (i + d) % blocks
                value = jnp.dot(rows, slab[:, j * NB : (j + 1) * NB], preferred_element_type=F32)
                for c in range(2):
                    band[i // 4, i // 2 % 2, i % 2, c, :, d * NB : (d + 1) * NB] = value[
                        c * NB // 2 : (c + 1) * NB // 2
                    ]
        hops[0].start()
        hops[0].wait()
        for c in range(2):
            @pl.when(core == c)
            def _():
                sums[...] = band[:, :, :, c] + first[...]
        hops[1].start()
        hops[1].wait()
        for c in range(2):
            @pl.when(x == c)
            def _():
                second[...] = second[...] + sums[:, :, c]
        hops[2].start()
        hops[2].wait()
        for c in range(2):
            @pl.when(low == c)
            def _():
                third[...] = third[...] + second[:, c]
        hops[3].start()
        hops[3].wait()
        for c in range(2):
            @pl.when(high == c)
            def _():
                fourth[...] = fourth[...] + third[c]
        hops[4].start()
        hops[4].wait_send()
        band_ref[...] = fourth[...]
        for h in range(2):
            masks[h].wait_send()

    @pl.when(order == 1)
    def _():
        for raw in raws:
            raw.start()
        for h in range(2):
            masks[h].wait_recv()
            swaps[h].start()
            keeps[h].start()
        hops[4].wait_recv()
        band_ref[...] = last[...]

    for h in range(2):
        swaps[h].wait()
        keeps[h].wait()
    for raw in raws:
        raw.wait()


def opening(design, arc_lengths, size):
    steps, ord_cols = design.shape
    group = NB // 2
    width = BAND * NB
    anywhere = pl.BlockSpec(memory_space=pl.ANY)
    sems = pltpu.SemaphoreType.DMA
    return pl.pallas_call(
        opening_kernel,
        out_shape=(
            jax.ShapeDtypeStruct((2, size // 2, steps), BF16),
            jax.ShapeDtypeStruct((2, size // 2, steps), BF16),
            jax.ShapeDtypeStruct((4, steps, ord_cols // 8), BF16),
            jax.ShapeDtypeStruct((group, width), F32),
        ),
        in_specs=[pl.BlockSpec(memory_space=pltpu.SMEM), anywhere],
        out_specs=(anywhere, anywhere, anywhere, pl.BlockSpec(memory_space=pltpu.VMEM)),
        scratch_shapes=[
            pltpu.VMEM((steps, size), BF16),
            pltpu.VMEM((2, size // 2, steps), BF16),
            pltpu.VMEM((2, 2, 2, 2, group, width), F32),
            pltpu.VMEM((2, 2, 2, group, width), F32),
            pltpu.VMEM((2, 2, 2, group, width), F32),
            pltpu.VMEM((2, 2, group, width), F32),
            pltpu.VMEM((2, group, width), F32),
            pltpu.VMEM((group, width), F32),
            pltpu.VMEM((group, width), F32),
            sems((3,)), sems((4,)), sems((4,)), sems((2,)), sems((2,)), sems((2,)), sems((2,)),
            sems((5,)), sems((5,)),
        ],
        compiler_params=pltpu.CompilerParams(
            vmem_limit_bytes=VMEM_BYTES, collective_id=0, has_side_effects=True
        ),
        cost_estimate=cost(60_000_000_000, 48 << 20),
    )(arc_lengths, design)


def encode(value, group):
    height, width = value.shape
    grouped = value.reshape(height // group, group, width)
    top = jnp.max(jnp.abs(grouped), axis=1)
    index = jnp.ceil(jnp.log2(jnp.maximum(top, 1e-30)) * 8.0)
    factor = jnp.exp2(index * -0.125) * LEVELS
    code = jnp.round(grouped * factor[:, None, :]).astype(jnp.int32).astype(jnp.int16)
    return code.reshape(height, width), index


def decode(code, index, group):
    height, width = code.shape
    step = jnp.exp2(index * 0.125) * (1.0 / LEVELS)
    grouped = code.astype(jnp.int32).astype(F32).reshape(height // group, group, width)
    return (grouped * step[:, None, :]).reshape(height, width)


def stage_kernel(extra, coded, where_ref, own_ref, other_ref, mine_ref, theirs_ref, *rest):
    arrived, out_ref = rest[:extra], rest[extra]
    size = own_ref.shape[1]
    total = jnp.dot(own_ref[0], mine_ref[...], preferred_element_type=F32)
    total = total + jnp.dot(other_ref[0], theirs_ref[0], preferred_element_type=F32)
    groups = size // GROUP
    for ref in arrived:
        total = total + received(ref, size)
    if coded:
        code, index = encode(total, GROUP)
        out_ref[:size, :] = code
        index = jnp.concatenate([index, jnp.zeros((PAD - groups, index.shape[1]), F32)], axis=0)
        out_ref[size:, :] = index.astype(jnp.int32).astype(jnp.int16)
    else:
        out_ref[...] = total


def stage(masked, masked_other, design, others, h, k, block, other_block, width, arrived=(), coded=True):
    _, size, steps = masked.shape
    per = width // COLS
    height = size + PAD if coded else size
    whole = pl.BlockSpec((1, size, steps), lambda j, s: (h, 0, 0))
    code_spec = pl.BlockSpec((size + PAD, COLS), lambda j, s: (0, j))
    return pl.pallas_call(
        functools.partial(stage_kernel, len(arrived), coded),
        out_shape=jax.ShapeDtypeStruct((height, width), jnp.int16 if coded else F32),
        grid_spec=pltpu.PrefetchScalarGridSpec(
            num_scalar_prefetch=1,
            grid=(per,),
            in_specs=[
                whole,
                whole,
                pl.BlockSpec((steps, COLS), lambda j, s: (0, s[0] * per + j)),
                pl.BlockSpec((1, steps, COLS), lambda j, s: (k, 0, s[1] * per + j)),
            ]
            + [code_spec] * len(arrived),
            out_specs=pl.BlockSpec((height, COLS), lambda j, s: (0, j)),
        ),
        compiler_params=params(),
        cost_estimate=cost(4 * size * steps * width, (8 << 20) + 2 * height * width),
    )(jnp.stack([block, other_block]).astype(jnp.int32), masked, masked_other, design, others, *arrived)


def split(value):
    high = value.astype(BF16)
    return high, (value - high.astype(F32)).astype(BF16)


def received(ref, size):
    index = ref[size:, :].astype(jnp.int32).astype(F32)[: size // GROUP]
    return decode(ref[:size, :], index, GROUP)


def share_kernel(scale, group, flag_ref, inverse_ref, upper_ref, *rest):
    parts, (code_ref, index_ref) = rest[:-2], rest[-2:]
    size = inverse_ref.shape[0]
    chunk = 256
    use_upper = flag_ref[0] == 1
    highs, lows = [], []
    for h in range(2):
        own, *arrived = parts[h::2]
        value = own[...]
        for ref in arrived:
            value = value + received(ref, size // 2)
        high, low = split(value * scale)
        highs.append(high)
        lows.append(low)
    high, low = jnp.concatenate(highs, axis=0), jnp.concatenate(lows, axis=0)
    for i in range(size // chunk):
        here = slice(i * chunk, (i + 1) * chunk)
        depth = (i + 1) * chunk
        a_high, a_low = split(inverse_ref[here, :depth])
        value = jnp.dot(a_high, high[:depth], preferred_element_type=F32)
        value = value + jnp.dot(a_high, low[:depth], preferred_element_type=F32)
        value = value + jnp.dot(a_low, high[:depth], preferred_element_type=F32)
        value = jnp.where(use_upper, upper_ref[here, :], value)
        code, index = encode(value, group)
        per = chunk // group
        for g in range(per):
            code_ref[i * per + g] = code[g * group : (g + 1) * group]
            index_ref[i * per + g] = index[g : g + 1].astype(jnp.int32).astype(jnp.int16)


def share_of(inverse, upper, parts, holds_gram, scale, arcs):
    size, width = inverse.shape[0], parts[0].shape[1]
    group = size // arcs
    return pl.pallas_call(
        functools.partial(share_kernel, scale, group),
        out_shape=(
            jax.ShapeDtypeStruct((arcs, group, width), jnp.int16),
            jax.ShapeDtypeStruct((arcs, 1, width), jnp.int16),
        ),
        grid=(width // COLS,),
        in_specs=[
            pl.BlockSpec(memory_space=pltpu.SMEM),
            pl.BlockSpec((size, size), lambda j: (0, 0)),
            pl.BlockSpec((size, COLS), lambda j: (0, j)),
        ]
        + [pl.BlockSpec((part.shape[0], COLS), lambda j: (0, j)) for part in parts],
        out_specs=(
            pl.BlockSpec((arcs, group, COLS), lambda j: (0, 0, j)),
            pl.BlockSpec((arcs, 1, COLS), lambda j: (0, 0, j)),
        ),
        compiler_params=params(),
        cost_estimate=cost(6 * size * size * width, 14 << 20),
    )(holds_gram.astype(jnp.int32).reshape(1), inverse, upper, *parts)


def decode_kernel(code_ref, index_ref, out_ref):
    index = index_ref[0].astype(jnp.int32).astype(F32)
    step = jnp.exp2(index * 0.125) * (1.0 / LEVELS)
    out_ref[...] = code_ref[0].astype(jnp.int32).astype(F32) * step


def decode_rows(code, index):
    arcs, group, width = code.shape
    half = arcs // 2
    return pl.pallas_call(
        decode_kernel,
        out_shape=jax.ShapeDtypeStruct((group, arcs * width), F32),
        grid=(arcs,),
        in_specs=[
            pl.BlockSpec((1, group, width), lambda j: (j % half * 2 + j // half, 0, 0)),
            pl.BlockSpec((1, 1, width), lambda j: (j % half * 2 + j // half, 0, 0)),
        ],
        out_specs=pl.BlockSpec((group, width), lambda j: (0, j)),
        compiler_params=params(),
        cost_estimate=cost(2 * arcs * group * width, 6 << 20),
    )(code, index)


def send(value, bit):
    size = lax.axis_size("arc")
    return lax.ppermute(value, "arc", [(i, i ^ bit) for i in range(size)])


def on_device_paired(design, arc_lengths, kaula_prior):
    obs_dev, ord_cols = design.shape
    arcs = lax.axis_size("arc")
    slab_rows = TILE * PANELS
    width = ord_cols // arcs
    me = lax.axis_index("arc")
    order = lax.axis_index("ord")
    core, x, z = me % 2, (me // 2) % 2, me // 4
    inverse_norm = 1.0 / math.sqrt(arcs * obs_dev)

    def place(k, flip, c):
        return (c * (arcs // 4) + (z ^ k)) * 2 + (x ^ flip)

    masked, masked_other, others, reduced = opening(design, arc_lengths, slab_rows)
    band = lax.all_gather(reduced, "arc", axis=0, tiled=True)
    inverse, upper = factorize(band, kaula_prior, inverse_norm)

    def run(h, k, flip, pieces=(), coded=True):
        return stage(
            masked, masked_other, design, others, h, k,
            place(k, flip, core), x ^ flip, width, pieces, coded
        )

    away = [{k: run(h, k, 1) for k in (3, 2, 1, 0)} for h in range(2)]
    across = [{k: send(away[h][k], 2) for k in (3, 2, 1, 0)} for h in range(2)]

    own, from_two, from_one = [], [], []
    for h in range(2):
        from_three = send(run(h, 3, 0, (across[h][3],)), 4)
        from_two.append(send(run(h, 2, 0, (across[h][2], from_three)), 8))
        from_one.append(send(run(h, 1, 0, (across[h][1],)), 4))
        own.append(run(h, 0, 0, (across[h][0],), coded=False))

    holds_gram = (order == 0) & (me == 0)
    parts = own + from_two + from_one
    code, index = share_of(inverse, upper, parts, holds_gram, inverse_norm, arcs)
    code = lax.all_to_all(code, "arc", split_axis=0, concat_axis=0, tiled=True)
    index = lax.all_to_all(index, "arc", split_axis=0, concat_axis=0, tiled=True)
    return decode_rows(code, index)


def solution(mesh):
    in_specs = (P("arc", "ord"), P("arc"), P())
    out_specs = P("arc", "ord")
    paired = mesh.shape["arc"] == 16 and mesh.shape["ord"] == 2
    return jax.shard_map(
        on_device_paired if paired else on_device,
        mesh=mesh, in_specs=in_specs, out_specs=out_specs, check_vma=False
    )
```

```python
import functools
import math

import jax
import jax.numpy as jnp
from jax import lax
from jax.experimental import pallas as pl
from jax.experimental.pallas import tpu as pltpu
from jax.sharding import PartitionSpec as P

TILE = 512
PANELS = 2


def broadcast(block, axis, source):
    block = jnp.where(lax.axis_index(axis) == source, block, jnp.zeros_like(block))
    return lax.psum(block, axis)


def apply_panels(matrix, lowers, couplings):
    blocks = [matrix[p * TILE : (p + 1) * TILE] for p in range(PANELS)]
    for p in range(PANELS):
        blocks[p] = jax.scipy.linalg.solve_triangular(lowers[p], blocks[p], lower=True)
        for q in range(p + 1, PANELS):
            blocks[q] = blocks[q] - jnp.dot(
                couplings[p, q].T, blocks[p], precision=lax.Precision.HIGHEST
            )
    return jnp.concatenate(blocks, axis=0)


def on_device(design, arc_lengths, kaula_prior):
    obs_dev, ord_cols = design.shape
    arcs_here = arc_lengths.shape[0]
    arc_steps = obs_dev // arcs_here
    row_block = min(256, arc_steps)
    slab_rows = TILE * PANELS
    pieces = []
    for panel_index in range(PANELS):
        owner = panel_index * TILE // ord_cols
        offset = panel_index * TILE % ord_cols
        piece = design[:, offset : offset + TILE]
        pieces.append(broadcast(piece, "ord", owner))
    slab_cols = jnp.concatenate(pieces, axis=1)
    position = lax.broadcasted_iota(jnp.int32, (row_block, 1), 0)
    partial_value = jnp.zeros((slab_rows, ord_cols), jnp.float32)
    gram_part = jnp.zeros((slab_rows, slab_rows), jnp.float32)
    arc_slot = 0
    length = arc_lengths[arc_slot]
    blocks_live = (length + row_block - 1) // row_block

    def accumulate(step_idx, running, arc_slot=arc_slot, length=length):
        first_row = arc_slot * arc_steps + step_idx * row_block
        slab_block = lax.dynamic_slice_in_dim(slab_cols, first_row, row_block, 0)
        tile_block = lax.dynamic_slice_in_dim(design, first_row, row_block, 0)
        is_live = position + step_idx * row_block < length
        live_block = jnp.where(is_live, slab_block, jnp.zeros((), slab_block.dtype))
        dims = (((0,), (0,)), ((), ()))
        normal_acc = running[0] + lax.dot_general(
            live_block, tile_block, dims, preferred_element_type=jnp.float32
        )
        gram_acc = running[1] + lax.dot_general(
            live_block, slab_block, dims, preferred_element_type=jnp.float32
        )
        return (normal_acc, gram_acc)

    partial_value, gram_part = lax.fori_loop(0, blocks_live, accumulate, (partial_value, gram_part))
    inverse_norm = 1.0 / math.sqrt(lax.axis_size("arc") * obs_dev)
    square_ids = lax.broadcasted_iota(jnp.int32, (slab_rows, slab_rows), 0)
    square_cols = lax.broadcasted_iota(jnp.int32, (slab_rows, slab_rows), 1)
    gram = lax.psum(gram_part, "arc") * inverse_norm
    gram = gram + jnp.where(square_ids == square_cols, kaula_prior[:, None], 0.0)
    gram_blocks = [gram[p * TILE : (p + 1) * TILE] for p in range(PANELS)]
    lowers = []
    couplings = {}
    for p in range(PANELS):
        lower_factor = jnp.linalg.cholesky(gram_blocks[p][:, p * TILE : (p + 1) * TILE])
        lowers.append(lower_factor)
        gram_blocks[p] = jax.scipy.linalg.solve_triangular(lower_factor, gram_blocks[p], lower=True)
        for q in range(p + 1, PANELS):
            upper_tile = gram_blocks[p][:, q * TILE : (q + 1) * TILE]
            couplings[p, q] = upper_tile
            gram_blocks[q] = gram_blocks[q] - jnp.dot(
                upper_tile.T, gram_blocks[p], precision=lax.Precision.HIGHEST
            )
    row_index = lax.broadcasted_iota(jnp.int32, (slab_rows, 1), 0)
    summed = lax.psum_scatter(partial_value, "arc", scatter_dimension=1, tiled=True) * inverse_norm
    width = ord_cols // lax.axis_size("arc")
    col_first = lax.axis_index("ord") * ord_cols + lax.axis_index("arc") * width
    global_col = col_first + lax.broadcasted_iota(jnp.int32, (1, width), 1)
    matrix = summed + jnp.where(row_index == global_col, kaula_prior[:, None], 0.0)
    share = apply_panels(matrix, lowers, couplings)
    factor = lax.all_to_all(share, "arc", split_axis=0, concat_axis=1, tiled=True)
    return factor


NB = 128
BAND = 5
GROUP = 64
LEVELS = 32760.0
PAD = 16
COLS = 256
VMEM_BYTES = 60 << 20
F32 = jnp.float32
BF16 = jnp.bfloat16


def params():
    return pltpu.CompilerParams(vmem_limit_bytes=VMEM_BYTES)


def cost(flops, moved):
    return pl.CostEstimate(flops=flops, bytes_accessed=moved, transcendentals=0)


def tree_sum(terms):
    while len(terms) > 1:
        pairs = [terms[i] + terms[i + 1] for i in range(0, len(terms) - 1, 2)]
        terms = pairs + ([terms[-1]] if len(terms) % 2 else [])
    return terms[0]


def diagonal_inverse(block):
    tiles = NB // 8
    sub = lax.broadcasted_iota(jnp.int32, (8, NB), 0)
    lane = lax.broadcasted_iota(jnp.int32, (8, NB), 1)
    rest = [block[8 * t : 8 * t + 8] for t in range(tiles)]
    inv = [jnp.where(sub + 8 * t == lane, 1.0, 0.0).astype(F32) for t in range(tiles)]

    def lanes(value, j):
        return jnp.broadcast_to(value[:, j : j + 1], (8, NB))

    def rows(value):
        return [jnp.broadcast_to(value[s : s + 1], (8, NB)) for s in range(8)]

    def combine(columns, row_values):
        return tree_sum([c * r for c, r in zip(columns, row_values)])

    for t in range(tiles):
        column = [lanes(rest[t], 8 * t + s) for s in range(8)]
        unit = [jnp.where(sub == s, 1.0, 0.0).astype(F32) for s in range(8)]
        whole = list(unit)
        pivots = jnp.ones((8, NB), F32)
        for s in range(8):
            pivot = jnp.broadcast_to(column[s][s : s + 1], (8, NB))
            recip = 1.0 / pivot
            pivots = jnp.where(sub == s, pivot, pivots)
            scaled = column[s] * recip
            below = jnp.where(sub > s, scaled, 0.0)
            others = jnp.where(sub == s, 1.0 - recip, scaled)
            for q in range(s + 1, 8):
                column[q] = column[q] - others * jnp.broadcast_to(column[q][s : s + 1], (8, NB))
            for q in range(s + 1):
                whole[q] = whole[q] - others * jnp.broadcast_to(whole[q][s : s + 1], (8, NB))
                unit[q] = unit[q] - below * jnp.broadcast_to(unit[q][s : s + 1], (8, NB))
        inv_rows = rows(inv[t])
        if t + 1 < tiles:
            solved = rows(combine(whole, rows(rest[t])))
            inv_solved = rows(combine(whole, inv_rows))
            for i in range(t + 1, tiles):
                columns = [lanes(rest[i], 8 * t + s) for s in range(8)]
                rest[i] = rest[i] - combine(columns, solved)
                inv[i] = inv[i] - combine(columns, inv_solved)
        inv[t] = combine(unit, inv_rows) * (1.0 / jnp.sqrt(pivots))
    return jnp.concatenate(inv, axis=0)


def exact_dot(a, b):
    return jnp.dot(a, b, precision=lax.Precision.HIGHEST)


def encode(value, group):
    height, width = value.shape
    grouped = value.reshape(height // group, group, width)
    top = jnp.max(jnp.abs(grouped), axis=1)
    index = jnp.ceil(jnp.log2(jnp.maximum(top, 1e-30)) * 8.0)
    factor = jnp.exp2(index * -0.125) * LEVELS
    code = jnp.round(grouped * factor[:, None, :]).astype(jnp.int32).astype(jnp.int16)
    return code.reshape(height, width), index


def decode(code, index, group):
    height, width = code.shape
    step = jnp.exp2(index * 0.125) * (1.0 / LEVELS)
    grouped = code.astype(jnp.int32).astype(F32).reshape(height // group, group, width)
    return (grouped * step[:, None, :]).reshape(height, width)


def levels(value, size):
    return value.astype(jnp.int32).astype(F32)[: size // GROUP]


def split(value):
    high = value.astype(BF16)
    return high, (value - high.astype(F32)).astype(BF16)


MESH = pl.DeviceIdType.MESH
WIDE = 512


def start_factor(gathered, prior_ref, work, scale):
    size = work.shape[0]
    blocks = size // NB
    sub = lax.broadcasted_iota(jnp.int32, (NB, NB), 0)
    lane = lax.broadcasted_iota(jnp.int32, (NB, NB), 1)
    eye = jnp.where(sub == lane, 1.0, 0.0).astype(F32)

    def band(i, d):
        parts = gathered[i // 4, i // 2 % 2, i % 2, :, :, d * NB : (d + 1) * NB]
        return parts.reshape(NB, NB)

    for i in range(blocks):
        here = slice(i * NB, (i + 1) * NB)
        for j in range(blocks):
            if j < i:
                value = jnp.zeros((NB, NB), F32)
            elif j - i < BAND:
                value = band(i, j - i) * scale
            else:
                value = band(j, i - j + blocks).T * scale
            if i == j:
                value = value + eye * prior_ref[i : i + 1, :]
            work[here, j * NB : (j + 1) * NB] = value


def factor_steps(first, last, work, upper, left):
    size = work.shape[0]
    blocks = size // NB
    sub = lax.broadcasted_iota(jnp.int32, (NB, NB), 0)
    lane = lax.broadcasted_iota(jnp.int32, (NB, NB), 1)
    eye = jnp.where(sub == lane, 1.0, 0.0).astype(F32)

    def step(k, carry):
        here = pl.ds(pl.multiple_of(k * NB, NB), NB)
        block = work[here, here]
        inverse = diagonal_inverse(block)
        work[here, here] = eye
        left[...] = exact_dot(inverse, work[here, :])
        column = lax.broadcasted_iota(jnp.int32, (NB, size), 1)
        upper[here, :] = jnp.where(column >= (k + 1) * NB, left[...], 0.0)
        upper[here, here] = exact_dot(inverse, block)
        work[here, :] = jnp.where(column < (k + 1) * NB, left[...], 0.0)

        def update(i, carry):
            there = pl.ds(pl.multiple_of(i * NB, NB), NB)
            work[there, here] = jnp.zeros((NB, NB), F32)
            work[there, :] -= exact_dot(left[:, there].T, left[...])
            return carry

        return lax.fori_loop(k + 1, blocks, update, carry)

    lax.fori_loop(first, last, step, 0)


def whole_kernel(
    scale,
    length_ref, design_ref, prior_ref, code_out, index_out, raw_ref,
    tiles, mask, other, band, first, sums, second, third, fourth, last, gathered,
    work, upper, left, away, across, upward, own, code, index,
    local_sem, tile_sem, raw_send, raw_recv, mask_send, mask_recv, swap_send, swap_recv,
    hop_send, hop_recv, gather_send, gather_recv, x_send, x_recv, z_send, z_recv,
    code_send, code_recv, index_send, index_recv,
):
    steps, ord_cols = design_ref.shape
    size = work.shape[0]
    blocks = size // NB
    arcs = code.shape[0]
    group = code.shape[1]
    rows = size // 2
    width = ord_cols // arcs
    me, order = lax.axis_index("arc"), lax.axis_index("ord")
    core, x, low, high = me % 2, me // 2 % 2, me // 4 % 2, me // 8
    peer = [
        (me + 1 - 2 * core, order),
        (me + 2 - 4 * x, order),
        (me + 4 - 8 * low, order),
        (me + 8 - 16 * high, order),
    ]
    opposite = (me, 1 - order)

    barrier = pltpu.get_barrier_semaphore()

    def greet(s, carry):
        device = (lax.rem(me + s, arcs), order)
        pl.semaphore_signal(barrier, inc=1, device_id=device, device_id_type=MESH)
        return carry

    lax.fori_loop(1, arcs, greet, 0)
    pl.semaphore_signal(barrier, inc=1, device_id=opposite, device_id_type=MESH)
    pl.semaphore_wait(barrier, arcs)

    def remote(source, target, send_sem, recv_sem, device):
        return pltpu.make_async_remote_copy(
            src_ref=source, dst_ref=target, send_sem=send_sem, recv_sem=recv_sem,
            device_id=device, device_id_type=MESH,
        )

    def place(k):
        z_high = high if k < 2 else 1 - high
        z_low = low if k % 2 == 0 else 1 - low
        return 2 * z_high + z_low

    raws = []
    for k in range(4):
        columns = pl.ds(pl.multiple_of(((1 - core) * 4 + place(k)) * 2 * width, width), 2 * width)
        raws.append(
            remote(design_ref.at[:, columns], raw_ref.at[k], raw_send.at[k], raw_recv.at[k], peer[0])
        )
    masks = [
        remote(mask.at[h], mask.at[h], mask_send.at[h], mask_recv.at[h], opposite) for h in range(2)
    ]
    swaps = [
        remote(mask.at[h], other.at[h], swap_send.at[h], swap_recv.at[h], peer[0]) for h in range(2)
    ]
    hops = [
        remote(band.at[:, :, :, 1 - core], first, hop_send.at[0], hop_recv.at[0], peer[0]),
        remote(sums.at[:, :, 1 - x], second, hop_send.at[1], hop_recv.at[1], peer[1]),
        remote(second.at[:, 1 - low], third, hop_send.at[2], hop_recv.at[2], peer[2]),
        remote(third.at[1 - high], fourth, hop_send.at[3], hop_recv.at[3], peer[3]),
        remote(fourth, last, hop_send.at[4], hop_recv.at[4], opposite),
    ]
    held = [
        (gathered.at[high, low, x, core], peer[1]),
        (gathered.at[high, low, :, core], peer[3]),
        (gathered.at[:, low, :, core], peer[2]),
        (gathered.at[:, :, :, core], peer[0]),
    ]
    gathers = [
        remote(part, part, gather_send.at[i], gather_recv.at[i], device)
        for i, (part, device) in enumerate(held)
    ]
    xs = [remote(away.at[n], across.at[n], x_send.at[n], x_recv.at[n], peer[1]) for n in range(8)]
    zs = [
        remote(
            away.at[4 * h + 3 - k], upward.at[3 * h + k - 1], z_send.at[3 * h + k - 1],
            z_recv.at[3 * h + k - 1], peer[3] if k == 2 else peer[2],
        )
        for h in range(2) for k in (1, 2, 3)
    ]

    stages = [(0, 3, 1), (0, 2, 1), (0, 1, 1), (0, 0, 1), (1, 3, 1), (0, 3, 0), (1, 2, 1), (0, 2, 0)]
    stages += [(0, 1, 0), (1, 1, 1), (0, 0, 0), (1, 0, 1), (1, 3, 0), (1, 2, 0), (1, 1, 0), (1, 0, 0)]

    def loads(n, t):
        _, k, flip = stages[n]
        block = x if flip == 0 else 1 - x
        mine = ((core * 4 + place(k)) * 2 + block) * width + t * WIDE
        theirs = block * width + t * WIDE
        return [
            pltpu.make_async_copy(
                design_ref.at[:, pl.ds(pl.multiple_of(mine, WIDE), WIDE)], tiles.at[t, 0], tile_sem.at[t, 0]
            ),
            pltpu.make_async_copy(
                raw_ref.at[k, :, pl.ds(pl.multiple_of(theirs, WIDE), WIDE)], tiles.at[t, 1], tile_sem.at[t, 1]
            ),
        ]

    def begin(n, t):
        if n < 4 and t == 0:
            raws[stages[n][1]].wait_recv()
        for load in loads(n, t):
            load.start()

    def stage(n, arrived, out, coded=True):
        h = stages[n][0]
        for t in range(width // WIDE):
            if t == 0:
                begin(n, 1)
            elif n + 1 < len(stages):
                begin(n + 1, 0)
            for load in loads(n, t):
                load.wait()

            def column(j, carry):
                part = pl.ds(pl.multiple_of(j * COLS, COLS), COLS)
                to = pl.ds(pl.multiple_of(t * WIDE + j * COLS, COLS), COLS)
                total = jnp.dot(mask[h], tiles[t, 0, :, part], preferred_element_type=F32)
                total = total + jnp.dot(other[h], tiles[t, 1, :, part], preferred_element_type=F32)
                for ref in arrived:
                    total = total + decode(ref[:rows, to], levels(ref[rows:, to], rows), GROUP)
                if coded:
                    value, level = encode(total, GROUP)
                    out[:rows, to] = value
                    level = jnp.concatenate([level, jnp.zeros((PAD - rows // GROUP, COLS), F32)], axis=0)
                    out[rows:, to] = level.astype(jnp.int32).astype(jnp.int16)
                else:
                    out[:, to] = total
                return carry

            lax.fori_loop(0, WIDE // COLS, column, 0)

    @pl.when(order == 0)
    def _():
        slab = [
            pltpu.make_async_copy(
                design_ref.at[:, pl.ds(c * WIDE, WIDE)], tiles.at[c, 0], local_sem.at[c]
            )
            for c in range(2)
        ]
        for load in slab:
            load.start()
        position = lax.broadcasted_iota(jnp.int32, (steps, NB), 0)
        per = blocks // 2
        for h in range(2):
            slab[h].wait()
            for i in range(per):
                piece = tiles[h, 0, :, i * NB : (i + 1) * NB].astype(F32)
                piece = jnp.where(position < length_ref[0], piece, 0.0)
                mask[h, i * NB : (i + 1) * NB, :] = piece.T.astype(BF16)
            masks[h].start()
            swaps[h].start()
            if h == 0:
                raws[3].start()
        for k in (2, 1, 0):
            raws[k].start()
        for i in range(blocks):
            lines = mask[i // per, i % per * NB : (i % per + 1) * NB, :]
            for d in range(BAND):
                j = (i + d) % blocks
                value = jnp.dot(
                    lines, tiles[j // per, 0, :, j % per * NB : (j % per + 1) * NB],
                    preferred_element_type=F32,
                )
                band[i // 4, i // 2 % 2, i % 2, :, :, d * NB : (d + 1) * NB] = value.reshape(
                    2, NB // 2, NB
                )
        hops[0].start()

    @pl.when(order == 1)
    def _():
        for k in (3, 2, 1, 0):
            raws[k].start()
        masks[0].wait_recv()
        swaps[0].start()

    def hop(step):
        @pl.when(order == 0)
        def _():
            hops[step].wait()
            if step == 0:
                sums[...] = band[:, :, :, core] + first[...]
            elif step == 1:
                second[...] = second[...] + sums[:, :, x]
            elif step == 2:
                third[...] = third[...] + second[:, low]
            else:
                fourth[...] = fourth[...] + third[high]
            hops[step + 1].start()

    def outgoing(n):
        h, k, _ = stages[n]
        stage(n, (), away.at[4 * h + 3 - k])

    def pump(m):
        xs[m].wait_send()
        if m + 2 < 8:
            xs[m + 2].start()

    def incoming(n):
        h, k, _ = stages[n]
        m = 4 * h + 3 - k
        xs[m].wait_recv()
        arrived = [across.at[m]]
        if k == 2:
            zs[3 * h + 2].wait_recv()
            arrived.append(upward.at[3 * h + 2])
        if k == 0:
            stage(n, arrived, own.at[h], coded=False)
        else:
            stage(n, arrived, away.at[m])
            zs[3 * h + k - 1].start()

    def steps_of(first, last):
        factor_steps(first, last, work, upper, left)

    begin(0, 0)
    hop(0)
    swaps[0].wait_recv()
    outgoing(0)
    xs[0].start()
    hop(1)
    outgoing(1)
    xs[1].start()
    hop(2)
    outgoing(2)
    hop(3)

    @pl.when(order == 0)
    def _():
        hops[4].wait_send()
        gathered[high, low, x, core] = fourth[...]

    @pl.when(order == 1)
    def _():
        masks[1].wait_recv()
        swaps[1].start()
        hops[4].wait_recv()
        gathered[high, low, x, core] = last[...]

    gathers[0].start()
    outgoing(3)
    gathers[0].wait()
    gathers[1].start()
    swaps[1].wait_recv()
    outgoing(4)
    gathers[1].wait()
    gathers[2].start()
    pump(0)
    incoming(5)
    gathers[2].wait()
    gathers[3].start()
    outgoing(6)
    pump(1)
    gathers[3].wait()
    start_factor(gathered, prior_ref, work, scale)
    steps_of(0, 1)
    pump(2)
    incoming(7)
    incoming(8)
    outgoing(9)
    steps_of(1, 3)
    pump(3)
    incoming(10)
    outgoing(11)
    steps_of(3, 4)
    pump(4)
    incoming(12)
    steps_of(4, 6)
    pump(5)
    incoming(13)
    steps_of(6, 8)
    pump(6)
    incoming(14)
    pump(7)
    incoming(15)
    for h in range(2):
        zs[3 * h].wait_recv()
        zs[3 * h + 1].wait_recv()

    use_upper = jnp.logical_and(order == 0, me == 0)
    chunk = 2 * NB

    def code_copy(half, s):
        to = lax.rem(me + s, arcs)
        columns = pl.ds(half * WIDE, WIDE)
        return remote(
            code.at[to, :, columns], code_out.at[me, :, columns],
            code_send.at[half, s - 1], code_recv.at[half, s - 1], (to, order),
        )

    def index_copy(s):
        to = lax.rem(me + s, arcs)
        return remote(
            index.at[to], index_out.at[me], index_send.at[s - 1], index_recv.at[s - 1], (to, order)
        )

    for half in range(2):
        def column(j, carry):
            to = pl.ds(pl.multiple_of(half * WIDE + j * COLS, COLS), COLS)
            highs, lows = [], []
            for h in range(2):
                value = own[h, :, to]
                for ref in (upward.at[3 * h], upward.at[3 * h + 1]):
                    value = value + decode(ref[:rows, to], levels(ref[rows:, to], rows), GROUP)
                top, rest = split(value * scale)
                highs.append(top)
                lows.append(rest)
            top, rest = jnp.concatenate(highs, axis=0), jnp.concatenate(lows, axis=0)
            for i in range(size // chunk):
                here = slice(i * chunk, (i + 1) * chunk)
                depth = (i + 1) * chunk
                a_top, a_rest = split(work[here, :depth])
                value = jnp.dot(a_top, top[:depth], preferred_element_type=F32)
                value = value + jnp.dot(a_top, rest[:depth], preferred_element_type=F32)
                value = value + jnp.dot(a_rest, top[:depth], preferred_element_type=F32)
                value = jnp.where(use_upper, upper[here, to], value)
                codes, level = encode(value, group)
                for g in range(chunk // group):
                    code[i * (chunk // group) + g, :, to] = codes[g * group : (g + 1) * group]
                    index[i * (chunk // group) + g, :, to] = level[g : g + 1]
            return carry

        lax.fori_loop(0, WIDE // COLS, column, 0)

        def launch(s, carry):
            code_copy(half, s).start()
            return carry

        lax.fori_loop(1, arcs, launch, 0)

    def launch_index(s, carry):
        index_copy(s).start()
        return carry

    lax.fori_loop(1, arcs, launch_index, 0)
    keeps = [
        pltpu.make_async_copy(code.at[me], code_out.at[me], local_sem.at[0]),
        pltpu.make_async_copy(index.at[me], index_out.at[me], local_sem.at[1]),
    ]
    for keep in keeps:
        keep.start()

    @pl.when(order == 0)
    def _():
        for h in range(2):
            masks[h].wait_send()
    for h in range(2):
        swaps[h].wait_send()
    for raw in raws:
        raw.wait_send()
    for z in zs:
        z.wait_send()

    def finish(s, carry):
        for half in range(2):
            code_copy(half, s).wait()
        index_copy(s).wait()
        return carry

    lax.fori_loop(1, arcs, finish, 0)
    for keep in keeps:
        keep.wait()


def whole(design, arc_lengths, prior, size, arcs, scale):
    steps, ord_cols = design.shape
    width = ord_cols // arcs
    group = NB // 2
    span = BAND * NB
    rows = size // 2
    anywhere = pl.BlockSpec(memory_space=pl.ANY)
    sems = pltpu.SemaphoreType.DMA
    vmem = pltpu.VMEM
    int16 = jnp.int16
    code, index, _ = pl.pallas_call(
        functools.partial(whole_kernel, scale),
        out_shape=(
            jax.ShapeDtypeStruct((arcs, size // arcs, width), int16),
            jax.ShapeDtypeStruct((arcs, 1, width), F32),
            jax.ShapeDtypeStruct((4, steps, 2 * width), BF16),
        ),
        in_specs=[pl.BlockSpec(memory_space=pltpu.SMEM), anywhere, pl.BlockSpec(memory_space=vmem)],
        out_specs=(anywhere, anywhere, anywhere),
        scratch_shapes=[
            vmem((2, 2, steps, WIDE), BF16),
            vmem((2, rows, steps), BF16),
            vmem((2, rows, steps), BF16),
            vmem((2, 2, 2, 2, group, span), F32),
            vmem((2, 2, 2, group, span), F32),
            vmem((2, 2, 2, group, span), F32),
            vmem((2, 2, group, span), F32),
            vmem((2, group, span), F32),
            vmem((group, span), F32),
            vmem((group, span), F32),
            vmem((2, 2, 2, 2, group, span), F32),
            vmem((size, size), F32),
            vmem((size, size), F32),
            vmem((NB, size), F32),
            vmem((8, rows + PAD, width), int16),
            vmem((8, rows + PAD, width), int16),
            vmem((6, rows + PAD, width), int16),
            vmem((2, rows, width), F32),
            vmem((arcs, size // arcs, width), int16),
            vmem((arcs, 1, width), F32),
            sems((2,)), sems((2, 2)), sems((4,)), sems((4,)), sems((2,)), sems((2,)), sems((2,)), sems((2,)),
            sems((5,)), sems((5,)), sems((4,)), sems((4,)), sems((8,)), sems((8,)), sems((6,)), sems((6,)),
            sems((2, arcs - 1)), sems((2, arcs - 1)), sems((arcs - 1,)), sems((arcs - 1,)),
        ],
        compiler_params=pltpu.CompilerParams(
            vmem_limit_bytes=VMEM_BYTES, collective_id=0, has_side_effects=True
        ),
        cost_estimate=cost(300_000_000_000, 100 << 20),
    )(arc_lengths, design, prior.reshape(size // NB, NB))
    return code, index


def decode_kernel(code_ref, index_ref, out_ref):
    chips, _, group, width = code_ref.shape
    for c in range(chips):
        step = jnp.exp2(index_ref[c, 0] * 0.125) * (1.0 / LEVELS)
        out_ref[:, c * width : (c + 1) * width] = code_ref[c, 0].astype(jnp.int32).astype(F32) * step


def decode_rows(code, index):
    arcs, group, width = code.shape
    half, per = arcs // 2, 4
    place = lambda j: (j % (half // per), j // (half // per), 0, 0)
    return pl.pallas_call(
        decode_kernel,
        out_shape=jax.ShapeDtypeStruct((group, arcs * width), F32),
        grid=(arcs // per,),
        in_specs=[
            pl.BlockSpec((per, 1, group, width), place),
            pl.BlockSpec((per, 1, 1, width), place),
        ],
        out_specs=pl.BlockSpec((group, per * width), lambda j: (0, j)),
        compiler_params=params(),
        cost_estimate=cost(2 * arcs * group * width, 6 << 20),
    )(code.reshape(half, 2, group, width), index.reshape(half, 2, 1, width))


def on_device_paired(design, arc_lengths, kaula_prior):
    arcs = lax.axis_size("arc")
    inverse_norm = 1.0 / math.sqrt(arcs * design.shape[0])
    code, index = whole(design, arc_lengths, kaula_prior, TILE * PANELS, arcs, inverse_norm)
    return decode_rows(code, index)


def solution(mesh):
    in_specs = (P("arc", "ord"), P("arc"), P())
    out_specs = P("arc", "ord")
    paired = mesh.shape["arc"] == 16 and mesh.shape["ord"] == 2
    return jax.shard_map(
        on_device_paired if paired else on_device,
        mesh=mesh, in_specs=in_specs, out_specs=out_specs, check_vma=False
    )
```

```python
import functools
import math

import jax
import jax.numpy as jnp
from jax import lax
from jax.experimental import pallas as pl
from jax.experimental.pallas import tpu as pltpu
from jax.sharding import PartitionSpec as P

TILE = 512
PANELS = 2


def broadcast(block, axis, source):
    block = jnp.where(lax.axis_index(axis) == source, block, jnp.zeros_like(block))
    return lax.psum(block, axis)


def apply_panels(matrix, lowers, couplings):
    blocks = [matrix[p * TILE : (p + 1) * TILE] for p in range(PANELS)]
    for p in range(PANELS):
        blocks[p] = jax.scipy.linalg.solve_triangular(lowers[p], blocks[p], lower=True)
        for q in range(p + 1, PANELS):
            blocks[q] = blocks[q] - jnp.dot(
                couplings[p, q].T, blocks[p], precision=lax.Precision.HIGHEST
            )
    return jnp.concatenate(blocks, axis=0)


def on_device(design, arc_lengths, kaula_prior):
    obs_dev, ord_cols = design.shape
    arcs_here = arc_lengths.shape[0]
    arc_steps = obs_dev // arcs_here
    row_block = min(256, arc_steps)
    slab_rows = TILE * PANELS
    pieces = []
    for panel_index in range(PANELS):
        owner = panel_index * TILE // ord_cols
        offset = panel_index * TILE % ord_cols
        piece = design[:, offset : offset + TILE]
        pieces.append(broadcast(piece, "ord", owner))
    slab_cols = jnp.concatenate(pieces, axis=1)
    position = lax.broadcasted_iota(jnp.int32, (row_block, 1), 0)
    partial_value = jnp.zeros((slab_rows, ord_cols), jnp.float32)
    gram_part = jnp.zeros((slab_rows, slab_rows), jnp.float32)
    arc_slot = 0
    length = arc_lengths[arc_slot]
    blocks_live = (length + row_block - 1) // row_block

    def accumulate(step_idx, running, arc_slot=arc_slot, length=length):
        first_row = arc_slot * arc_steps + step_idx * row_block
        slab_block = lax.dynamic_slice_in_dim(slab_cols, first_row, row_block, 0)
        tile_block = lax.dynamic_slice_in_dim(design, first_row, row_block, 0)
        is_live = position + step_idx * row_block < length
        live_block = jnp.where(is_live, slab_block, jnp.zeros((), slab_block.dtype))
        dims = (((0,), (0,)), ((), ()))
        normal_acc = running[0] + lax.dot_general(
            live_block, tile_block, dims, preferred_element_type=jnp.float32
        )
        gram_acc = running[1] + lax.dot_general(
            live_block, slab_block, dims, preferred_element_type=jnp.float32
        )
        return (normal_acc, gram_acc)

    partial_value, gram_part = lax.fori_loop(0, blocks_live, accumulate, (partial_value, gram_part))
    inverse_norm = 1.0 / math.sqrt(lax.axis_size("arc") * obs_dev)
    square_ids = lax.broadcasted_iota(jnp.int32, (slab_rows, slab_rows), 0)
    square_cols = lax.broadcasted_iota(jnp.int32, (slab_rows, slab_rows), 1)
    gram = lax.psum(gram_part, "arc") * inverse_norm
    gram = gram + jnp.where(square_ids == square_cols, kaula_prior[:, None], 0.0)
    gram_blocks = [gram[p * TILE : (p + 1) * TILE] for p in range(PANELS)]
    lowers = []
    couplings = {}
    for p in range(PANELS):
        lower_factor = jnp.linalg.cholesky(gram_blocks[p][:, p * TILE : (p + 1) * TILE])
        lowers.append(lower_factor)
        gram_blocks[p] = jax.scipy.linalg.solve_triangular(lower_factor, gram_blocks[p], lower=True)
        for q in range(p + 1, PANELS):
            upper_tile = gram_blocks[p][:, q * TILE : (q + 1) * TILE]
            couplings[p, q] = upper_tile
            gram_blocks[q] = gram_blocks[q] - jnp.dot(
                upper_tile.T, gram_blocks[p], precision=lax.Precision.HIGHEST
            )
    row_index = lax.broadcasted_iota(jnp.int32, (slab_rows, 1), 0)
    summed = lax.psum_scatter(partial_value, "arc", scatter_dimension=1, tiled=True) * inverse_norm
    width = ord_cols // lax.axis_size("arc")
    col_first = lax.axis_index("ord") * ord_cols + lax.axis_index("arc") * width
    global_col = col_first + lax.broadcasted_iota(jnp.int32, (1, width), 1)
    matrix = summed + jnp.where(row_index == global_col, kaula_prior[:, None], 0.0)
    share = apply_panels(matrix, lowers, couplings)
    factor = lax.all_to_all(share, "arc", split_axis=0, concat_axis=1, tiled=True)
    return factor


NB = 128
BAND = 5
GROUP = 64
LEVELS = 32760.0
PAD = 16
COLS = 256
VMEM_BYTES = 60 << 20
F32 = jnp.float32
BF16 = jnp.bfloat16


def params():
    return pltpu.CompilerParams(vmem_limit_bytes=VMEM_BYTES)


def cost(flops, moved):
    return pl.CostEstimate(flops=flops, bytes_accessed=moved, transcendentals=0)


def tree_sum(terms):
    while len(terms) > 1:
        pairs = [terms[i] + terms[i + 1] for i in range(0, len(terms) - 1, 2)]
        terms = pairs + ([terms[-1]] if len(terms) % 2 else [])
    return terms[0]


def diagonal_inverse(block):
    tiles = NB // 8
    sub = lax.broadcasted_iota(jnp.int32, (8, NB), 0)
    lane = lax.broadcasted_iota(jnp.int32, (8, NB), 1)
    rest = [block[8 * t : 8 * t + 8] for t in range(tiles)]
    inv = [jnp.where(sub + 8 * t == lane, 1.0, 0.0).astype(F32) for t in range(tiles)]

    def lanes(value, j):
        return jnp.broadcast_to(value[:, j : j + 1], (8, NB))

    def rows(value):
        return [jnp.broadcast_to(value[s : s + 1], (8, NB)) for s in range(8)]

    def combine(columns, row_values):
        return tree_sum([c * r for c, r in zip(columns, row_values)])

    for t in range(tiles):
        column = [lanes(rest[t], 8 * t + s) for s in range(8)]
        unit = [jnp.where(sub == s, 1.0, 0.0).astype(F32) for s in range(8)]
        whole = list(unit)
        pivots = jnp.ones((8, NB), F32)
        for s in range(8):
            pivot = jnp.broadcast_to(column[s][s : s + 1], (8, NB))
            recip = 1.0 / pivot
            pivots = jnp.where(sub == s, pivot, pivots)
            scaled = column[s] * recip
            below = jnp.where(sub > s, scaled, 0.0)
            others = jnp.where(sub == s, 1.0 - recip, scaled)
            for q in range(s + 1, 8):
                column[q] = column[q] - others * jnp.broadcast_to(column[q][s : s + 1], (8, NB))
            for q in range(s + 1):
                whole[q] = whole[q] - others * jnp.broadcast_to(whole[q][s : s + 1], (8, NB))
                unit[q] = unit[q] - below * jnp.broadcast_to(unit[q][s : s + 1], (8, NB))
        inv_rows = rows(inv[t])
        if t + 1 < tiles:
            solved = rows(combine(whole, rows(rest[t])))
            inv_solved = rows(combine(whole, inv_rows))
            for i in range(t + 1, tiles):
                columns = [lanes(rest[i], 8 * t + s) for s in range(8)]
                rest[i] = rest[i] - combine(columns, solved)
                inv[i] = inv[i] - combine(columns, inv_solved)
        inv[t] = combine(unit, inv_rows) * (1.0 / jnp.sqrt(pivots))
    return jnp.concatenate(inv, axis=0)


def exact_dot(a, b):
    return jnp.dot(a, b, precision=lax.Precision.HIGHEST)


def encode(value, group):
    height, width = value.shape
    grouped = value.reshape(height // group, group, width)
    top = jnp.max(jnp.abs(grouped), axis=1)
    index = jnp.ceil(jnp.log2(jnp.maximum(top, 1e-30)) * 8.0)
    factor = jnp.exp2(index * -0.125) * LEVELS
    code = jnp.round(grouped * factor[:, None, :]).astype(jnp.int32).astype(jnp.int16)
    return code.reshape(height, width), index


def decode(code, index, group):
    height, width = code.shape
    step = jnp.exp2(index * 0.125) * (1.0 / LEVELS)
    grouped = code.astype(jnp.int32).astype(F32).reshape(height // group, group, width)
    return (grouped * step[:, None, :]).reshape(height, width)


def levels(value, size):
    return value.astype(jnp.int32).astype(F32)[: size // GROUP]


def split(value):
    high = value.astype(BF16)
    return high, (value - high.astype(F32)).astype(BF16)


MESH = pl.DeviceIdType.MESH
WIDE = 512


def start_factor(gathered, prior_ref, work, scale):
    size = work.shape[0]
    blocks = size // NB
    sub = lax.broadcasted_iota(jnp.int32, (NB, NB), 0)
    lane = lax.broadcasted_iota(jnp.int32, (NB, NB), 1)
    eye = jnp.where(sub == lane, 1.0, 0.0).astype(F32)

    def band(i, d):
        parts = gathered[i // 4, i // 2 % 2, i % 2, :, :, d * NB : (d + 1) * NB]
        return parts.reshape(NB, NB)

    for i in range(blocks):
        here = slice(i * NB, (i + 1) * NB)
        for j in range(blocks):
            if j < i:
                value = jnp.zeros((NB, NB), F32)
            elif j - i < BAND:
                value = band(i, j - i) * scale
            else:
                value = band(j, i - j + blocks).T * scale
            if i == j:
                value = value + eye * prior_ref[i : i + 1, :]
            work[here, j * NB : (j + 1) * NB] = value


def factor_steps(first, last, work, upper, left):
    size = work.shape[0]
    blocks = size // NB
    sub = lax.broadcasted_iota(jnp.int32, (NB, NB), 0)
    lane = lax.broadcasted_iota(jnp.int32, (NB, NB), 1)
    eye = jnp.where(sub == lane, 1.0, 0.0).astype(F32)

    def step(k, carry):
        here = pl.ds(pl.multiple_of(k * NB, NB), NB)
        block = work[here, here]
        inverse = diagonal_inverse(block)
        work[here, here] = eye
        left[...] = exact_dot(inverse, work[here, :])
        column = lax.broadcasted_iota(jnp.int32, (NB, size), 1)
        upper[here, :] = jnp.where(column >= (k + 1) * NB, left[...], 0.0)
        upper[here, here] = exact_dot(inverse, block)
        work[here, :] = jnp.where(column < (k + 1) * NB, left[...], 0.0)

        def update(i, carry):
            there = pl.ds(pl.multiple_of(i * NB, NB), NB)
            work[there, here] = jnp.zeros((NB, NB), F32)
            work[there, :] -= exact_dot(left[:, there].T, left[...])
            return carry

        return lax.fori_loop(k + 1, blocks, update, carry)

    lax.fori_loop(first, last, step, 0)


def whole_kernel(
    scale,
    length_ref, design_ref, prior_ref, code_out, index_out, raw_ref,
    tiles, mask, other, band, first, sums, second, third, fourth, last, gathered,
    work, upper, left, away, across, upward, own, code, index,
    local_sem, tile_sem, raw_send, raw_recv, mask_send, mask_recv, swap_send, swap_recv,
    hop_send, hop_recv, gather_send, gather_recv, x_send, x_recv, z_send, z_recv,
    code_send, code_recv, index_send, index_recv,
):
    steps, ord_cols = design_ref.shape
    size = work.shape[0]
    blocks = size // NB
    arcs = code.shape[0]
    group = code.shape[1]
    rows = size // 2
    width = ord_cols // arcs
    me, order = lax.axis_index("arc"), lax.axis_index("ord")
    core, x, low, high = me % 2, me // 2 % 2, me // 4 % 2, me // 8
    peer = [
        (me + 1 - 2 * core, order),
        (me + 2 - 4 * x, order),
        (me + 4 - 8 * low, order),
        (me + 8 - 16 * high, order),
    ]
    opposite = (me, 1 - order)

    barrier = pltpu.get_barrier_semaphore()

    def greet(s, carry):
        device = (lax.rem(me + s, arcs), order)
        pl.semaphore_signal(barrier, inc=1, device_id=device, device_id_type=MESH)
        return carry

    lax.fori_loop(1, arcs, greet, 0)
    pl.semaphore_signal(barrier, inc=1, device_id=opposite, device_id_type=MESH)
    pl.semaphore_wait(barrier, arcs)

    def remote(source, target, send_sem, recv_sem, device):
        return pltpu.make_async_remote_copy(
            src_ref=source, dst_ref=target, send_sem=send_sem, recv_sem=recv_sem,
            device_id=device, device_id_type=MESH,
        )

    def place(k):
        z_high = high if k < 2 else 1 - high
        z_low = low if k % 2 == 0 else 1 - low
        return 2 * z_high + z_low

    raws = []
    for k in range(4):
        columns = pl.ds(pl.multiple_of(((1 - core) * 4 + place(k)) * 2 * width, width), 2 * width)
        raws.append(
            remote(design_ref.at[:, columns], raw_ref.at[k], raw_send.at[k], raw_recv.at[k], peer[0])
        )
    masks = [
        remote(mask.at[h], mask.at[h], mask_send.at[h], mask_recv.at[h], opposite) for h in range(2)
    ]
    swaps = [
        remote(mask.at[h], other.at[h], swap_send.at[h], swap_recv.at[h], peer[0]) for h in range(2)
    ]
    hops = [
        remote(band.at[:, :, :, 1 - core], first, hop_send.at[0], hop_recv.at[0], peer[0]),
        remote(sums.at[:, :, 1 - x], second, hop_send.at[1], hop_recv.at[1], peer[1]),
        remote(second.at[:, 1 - low], third, hop_send.at[2], hop_recv.at[2], peer[2]),
        remote(third.at[1 - high], fourth, hop_send.at[3], hop_recv.at[3], peer[3]),
        remote(fourth, last, hop_send.at[4], hop_recv.at[4], opposite),
    ]
    held = [
        (gathered.at[high, low, x, core], peer[1]),
        (gathered.at[high, low, :, core], peer[3]),
        (gathered.at[:, low, :, core], peer[2]),
        (gathered.at[:, :, :, core], peer[0]),
    ]
    gathers = [
        remote(part, part, gather_send.at[i], gather_recv.at[i], device)
        for i, (part, device) in enumerate(held)
    ]
    xs = [remote(away.at[n], across.at[n], x_send.at[n], x_recv.at[n], peer[1]) for n in range(8)]
    message = {(0, 3): 0, (0, 2): 1, (1, 3): 2, (1, 2): 3, (0, 1): 4, (1, 1): 5, (0, 0): 6, (1, 0): 7}
    zs = [
        remote(
            away.at[message[h, k]], upward.at[3 * h + k - 1], z_send.at[3 * h + k - 1],
            z_recv.at[3 * h + k - 1], peer[3] if k == 2 else peer[2],
        )
        for h in range(2) for k in (1, 2, 3)
    ]

    stages = [(0, 3, 1), (0, 2, 1), (1, 3, 1), (1, 2, 1), (0, 3, 0), (0, 1, 1), (0, 2, 0), (1, 1, 1)]
    stages += [(1, 3, 0), (0, 0, 1), (1, 0, 1), (1, 2, 0), (0, 1, 0), (1, 1, 0), (0, 0, 0), (1, 0, 0)]
    fresh = {3: 0, 2: 1, 1: 5, 0: 9}

    def loads(n, t):
        _, k, flip = stages[n]
        block = x if flip == 0 else 1 - x
        mine = ((core * 4 + place(k)) * 2 + block) * width + t * WIDE
        theirs = block * width + t * WIDE
        return [
            pltpu.make_async_copy(
                design_ref.at[:, pl.ds(pl.multiple_of(mine, WIDE), WIDE)], tiles.at[t, 0], tile_sem.at[t, 0]
            ),
            pltpu.make_async_copy(
                raw_ref.at[k, :, pl.ds(pl.multiple_of(theirs, WIDE), WIDE)], tiles.at[t, 1], tile_sem.at[t, 1]
            ),
        ]

    def begin(n, t):
        if t == 0 and fresh[stages[n][1]] == n:
            raws[stages[n][1]].wait_recv()
        for load in loads(n, t):
            load.start()

    def stage(n, arrived, out, coded=True):
        h = stages[n][0]
        for t in range(width // WIDE):
            if t == 0:
                begin(n, 1)
            elif n + 1 < len(stages):
                begin(n + 1, 0)
            for load in loads(n, t):
                load.wait()

            def column(j, carry):
                part = pl.ds(pl.multiple_of(j * COLS, COLS), COLS)
                to = pl.ds(pl.multiple_of(t * WIDE + j * COLS, COLS), COLS)
                total = jnp.dot(mask[h], tiles[t, 0, :, part], preferred_element_type=F32)
                total = total + jnp.dot(other[h], tiles[t, 1, :, part], preferred_element_type=F32)
                for ref in arrived:
                    total = total + decode(ref[:rows, to], levels(ref[rows:, to], rows), GROUP)
                if coded:
                    value, level = encode(total, GROUP)
                    out[:rows, to] = value
                    level = jnp.concatenate([level, jnp.zeros((PAD - rows // GROUP, COLS), F32)], axis=0)
                    out[rows:, to] = level.astype(jnp.int32).astype(jnp.int16)
                else:
                    out[:, to] = total
                return carry

            lax.fori_loop(0, WIDE // COLS, column, 0)

    raws[3].start()

    @pl.when(order == 0)
    def _():
        slab = [
            pltpu.make_async_copy(
                design_ref.at[:, pl.ds(c * WIDE, WIDE)], tiles.at[c, 0], local_sem.at[c]
            )
            for c in range(2)
        ]
        for load in slab:
            load.start()
        position = lax.broadcasted_iota(jnp.int32, (steps, NB), 0)
        per = blocks // 2
        for h in range(2):
            slab[h].wait()
            for i in range(per):
                piece = tiles[h, 0, :, i * NB : (i + 1) * NB].astype(F32)
                piece = jnp.where(position < length_ref[0], piece, 0.0)
                mask[h, i * NB : (i + 1) * NB, :] = piece.T.astype(BF16)
            if h == 0:
                masks[0].start()
            swaps[h].start()
            if h == 0:
                raws[2].start()
        for i in range(blocks):
            lines = mask[i // per, i % per * NB : (i % per + 1) * NB, :]
            for d in range(BAND):
                j = (i + d) % blocks
                value = jnp.dot(
                    lines, tiles[j // per, 0, :, j % per * NB : (j % per + 1) * NB],
                    preferred_element_type=F32,
                )
                band[i // 4, i // 2 % 2, i % 2, :, :, d * NB : (d + 1) * NB] = value.reshape(
                    2, NB // 2, NB
                )
        hops[0].start()

    @pl.when(order == 1)
    def _():
        raws[2].start()
        masks[0].wait_recv()
        swaps[0].start()

    def hop(step):
        @pl.when(order == 0)
        def _():
            hops[step].wait()
            if step == 0:
                sums[...] = band[:, :, :, core] + first[...]
            elif step == 1:
                second[...] = second[...] + sums[:, :, x]
            elif step == 2:
                third[...] = third[...] + second[:, low]
            else:
                fourth[...] = fourth[...] + third[high]
            hops[step + 1].start()

    def outgoing(n):
        h, k, _ = stages[n]
        stage(n, (), away.at[message[h, k]])

    def pump(m):
        xs[m].wait_send()
        if m + 2 < 8:
            xs[m + 2].start()

    def incoming(n):
        h, k, _ = stages[n]
        m = message[h, k]
        xs[m].wait_recv()
        arrived = [across.at[m]]
        if k == 2:
            zs[3 * h + 2].wait_recv()
            arrived.append(upward.at[3 * h + 2])
        if k == 0:
            stage(n, arrived, own.at[h], coded=False)
        else:
            stage(n, arrived, away.at[m])
            zs[3 * h + k - 1].start()

    def steps_of(first, last):
        factor_steps(first, last, work, upper, left)

    begin(0, 0)
    hop(0)
    swaps[0].wait_recv()
    outgoing(0)
    xs[0].start()

    @pl.when(order == 0)
    def _():
        masks[0].wait_send()
        masks[1].start()

    hop(1)
    outgoing(1)
    xs[1].start()
    raws[1].start()
    raws[0].start()
    hop(2)
    hop(3)

    @pl.when(order == 0)
    def _():
        hops[4].wait_send()
        gathered[high, low, x, core] = fourth[...]

    @pl.when(order == 1)
    def _():
        masks[1].wait_recv()
        swaps[1].start()
        hops[4].wait_recv()
        gathered[high, low, x, core] = last[...]

    gathers[0].start()
    swaps[1].wait_recv()
    outgoing(2)
    gathers[0].wait()
    gathers[1].start()
    outgoing(3)
    pump(0)
    gathers[1].wait()
    gathers[2].start()
    incoming(4)
    gathers[2].wait()
    gathers[3].start()
    outgoing(5)
    pump(1)
    gathers[3].wait()
    start_factor(gathered, prior_ref, work, scale)
    steps_of(0, 1)
    incoming(6)
    outgoing(7)
    pump(2)
    incoming(8)
    steps_of(1, 3)
    pump(3)
    outgoing(9)
    outgoing(10)
    steps_of(3, 4)
    incoming(11)
    steps_of(4, 5)
    pump(4)
    incoming(12)
    steps_of(5, 6)
    pump(5)
    incoming(13)
    steps_of(6, 8)
    pump(6)
    incoming(14)
    pump(7)
    incoming(15)
    for h in range(2):
        zs[3 * h].wait_recv()
        zs[3 * h + 1].wait_recv()

    use_upper = jnp.logical_and(order == 0, me == 0)
    chunk = 2 * NB

    def code_copy(half, s):
        to = lax.rem(me + s, arcs)
        columns = pl.ds(half * WIDE, WIDE)
        return remote(
            code.at[to, :, columns], code_out.at[me, :, columns],
            code_send.at[half, s - 1], code_recv.at[half, s - 1], (to, order),
        )

    def index_copy(s):
        to = lax.rem(me + s, arcs)
        return remote(
            index.at[to], index_out.at[me], index_send.at[s - 1], index_recv.at[s - 1], (to, order)
        )

    for half in range(2):
        def column(j, carry):
            to = pl.ds(pl.multiple_of(half * WIDE + j * COLS, COLS), COLS)
            highs, lows = [], []
            for h in range(2):
                value = own[h, :, to]
                for ref in (upward.at[3 * h], upward.at[3 * h + 1]):
                    value = value + decode(ref[:rows, to], levels(ref[rows:, to], rows), GROUP)
                top, rest = split(value * scale)
                highs.append(top)
                lows.append(rest)
            top, rest = jnp.concatenate(highs, axis=0), jnp.concatenate(lows, axis=0)
            for i in range(size // chunk):
                here = slice(i * chunk, (i + 1) * chunk)
                depth = (i + 1) * chunk
                a_top, a_rest = split(work[here, :depth])
                value = jnp.dot(a_top, top[:depth], preferred_element_type=F32)
                value = value + jnp.dot(a_top, rest[:depth], preferred_element_type=F32)
                value = value + jnp.dot(a_rest, top[:depth], preferred_element_type=F32)
                value = jnp.where(use_upper, upper[here, to], value)
                codes, level = encode(value, group)
                for g in range(chunk // group):
                    code[i * (chunk // group) + g, :, to] = codes[g * group : (g + 1) * group]
                    index[i * (chunk // group) + g, :, to] = level[g : g + 1]
            return carry

        lax.fori_loop(0, WIDE // COLS, column, 0)

        def launch(s, carry):
            code_copy(half, s).start()
            return carry

        lax.fori_loop(1, arcs, launch, 0)

    def launch_index(s, carry):
        index_copy(s).start()
        return carry

    lax.fori_loop(1, arcs, launch_index, 0)
    keeps = [
        pltpu.make_async_copy(code.at[me], code_out.at[me], local_sem.at[0]),
        pltpu.make_async_copy(index.at[me], index_out.at[me], local_sem.at[1]),
    ]
    for keep in keeps:
        keep.start()

    @pl.when(order == 0)
    def _():
        masks[1].wait_send()

    for h in range(2):
        swaps[h].wait_send()
    for raw in raws:
        raw.wait_send()
    for z in zs:
        z.wait_send()

    def finish(s, carry):
        for half in range(2):
            code_copy(half, s).wait()
        index_copy(s).wait()
        return carry

    lax.fori_loop(1, arcs, finish, 0)
    for keep in keeps:
        keep.wait()


def whole(design, arc_lengths, prior, size, arcs, scale):
    steps, ord_cols = design.shape
    width = ord_cols // arcs
    group = NB // 2
    span = BAND * NB
    rows = size // 2
    anywhere = pl.BlockSpec(memory_space=pl.ANY)
    sems = pltpu.SemaphoreType.DMA
    vmem = pltpu.VMEM
    int16 = jnp.int16
    code, index, _ = pl.pallas_call(
        functools.partial(whole_kernel, scale),
        out_shape=(
            jax.ShapeDtypeStruct((arcs, size // arcs, width), int16),
            jax.ShapeDtypeStruct((arcs, 1, width), F32),
            jax.ShapeDtypeStruct((4, steps, 2 * width), BF16),
        ),
        in_specs=[pl.BlockSpec(memory_space=pltpu.SMEM), anywhere, pl.BlockSpec(memory_space=vmem)],
        out_specs=(anywhere, anywhere, anywhere),
        scratch_shapes=[
            vmem((2, 2, steps, WIDE), BF16),
            vmem((2, rows, steps), BF16),
            vmem((2, rows, steps), BF16),
            vmem((2, 2, 2, 2, group, span), F32),
            vmem((2, 2, 2, group, span), F32),
            vmem((2, 2, 2, group, span), F32),
            vmem((2, 2, group, span), F32),
            vmem((2, group, span), F32),
            vmem((group, span), F32),
            vmem((group, span), F32),
            vmem((2, 2, 2, 2, group, span), F32),
            vmem((size, size), F32),
            vmem((size, size), F32),
            vmem((NB, size), F32),
            vmem((8, rows + PAD, width), int16),
            vmem((8, rows + PAD, width), int16),
            vmem((6, rows + PAD, width), int16),
            vmem((2, rows, width), F32),
            vmem((arcs, size // arcs, width), int16),
            vmem((arcs, 1, width), F32),
            sems((2,)), sems((2, 2)), sems((4,)), sems((4,)), sems((2,)), sems((2,)), sems((2,)), sems((2,)),
            sems((5,)), sems((5,)), sems((4,)), sems((4,)), sems((8,)), sems((8,)), sems((6,)), sems((6,)),
            sems((2, arcs - 1)), sems((2, arcs - 1)), sems((arcs - 1,)), sems((arcs - 1,)),
        ],
        compiler_params=pltpu.CompilerParams(
            vmem_limit_bytes=VMEM_BYTES, collective_id=0, has_side_effects=True
        ),
        cost_estimate=cost(300_000_000_000, 100 << 20),
    )(arc_lengths, design, prior.reshape(size // NB, NB))
    return code, index


def decode_kernel(code_ref, index_ref, out_ref):
    chips, _, group, width = code_ref.shape
    for c in range(chips):
        step = jnp.exp2(index_ref[c, 0] * 0.125) * (1.0 / LEVELS)
        out_ref[:, c * width : (c + 1) * width] = code_ref[c, 0].astype(jnp.int32).astype(F32) * step


def decode_rows(code, index):
    arcs, group, width = code.shape
    half, per = arcs // 2, 4
    place = lambda j: (j % (half // per), j // (half // per), 0, 0)
    return pl.pallas_call(
        decode_kernel,
        out_shape=jax.ShapeDtypeStruct((group, arcs * width), F32),
        grid=(arcs // per,),
        in_specs=[
            pl.BlockSpec((per, 1, group, width), place),
            pl.BlockSpec((per, 1, 1, width), place),
        ],
        out_specs=pl.BlockSpec((group, per * width), lambda j: (0, j)),
        compiler_params=params(),
        cost_estimate=cost(2 * arcs * group * width, 6 << 20),
    )(code.reshape(half, 2, group, width), index.reshape(half, 2, 1, width))


def on_device_paired(design, arc_lengths, kaula_prior):
    arcs = lax.axis_size("arc")
    inverse_norm = 1.0 / math.sqrt(arcs * design.shape[0])
    code, index = whole(design, arc_lengths, kaula_prior, TILE * PANELS, arcs, inverse_norm)
    return decode_rows(code, index)


def solution(mesh):
    in_specs = (P("arc", "ord"), P("arc"), P())
    out_specs = P("arc", "ord")
    paired = mesh.shape["arc"] == 16 and mesh.shape["ord"] == 2
    return jax.shard_map(
        on_device_paired if paired else on_device,
        mesh=mesh, in_specs=in_specs, out_specs=out_specs, check_vma=False
    )
```

```python
import functools
import math

import jax
import jax.numpy as jnp
from jax import lax
from jax.experimental import pallas as pl
from jax.experimental.pallas import tpu as pltpu
from jax.sharding import PartitionSpec as P

TILE = 512
PANELS = 2


def broadcast(block, axis, source):
    block = jnp.where(lax.axis_index(axis) == source, block, jnp.zeros_like(block))
    return lax.psum(block, axis)


def apply_panels(matrix, lowers, couplings):
    blocks = [matrix[p * TILE : (p + 1) * TILE] for p in range(PANELS)]
    for p in range(PANELS):
        blocks[p] = jax.scipy.linalg.solve_triangular(lowers[p], blocks[p], lower=True)
        for q in range(p + 1, PANELS):
            blocks[q] = blocks[q] - jnp.dot(
                couplings[p, q].T, blocks[p], precision=lax.Precision.HIGHEST
            )
    return jnp.concatenate(blocks, axis=0)


def on_device(design, arc_lengths, kaula_prior):
    obs_dev, ord_cols = design.shape
    arcs_here = arc_lengths.shape[0]
    arc_steps = obs_dev // arcs_here
    row_block = min(256, arc_steps)
    slab_rows = TILE * PANELS
    pieces = []
    for panel_index in range(PANELS):
        owner = panel_index * TILE // ord_cols
        offset = panel_index * TILE % ord_cols
        piece = design[:, offset : offset + TILE]
        pieces.append(broadcast(piece, "ord", owner))
    slab_cols = jnp.concatenate(pieces, axis=1)
    position = lax.broadcasted_iota(jnp.int32, (row_block, 1), 0)
    partial_value = jnp.zeros((slab_rows, ord_cols), jnp.float32)
    gram_part = jnp.zeros((slab_rows, slab_rows), jnp.float32)
    arc_slot = 0
    length = arc_lengths[arc_slot]
    blocks_live = (length + row_block - 1) // row_block

    def accumulate(step_idx, running, arc_slot=arc_slot, length=length):
        first_row = arc_slot * arc_steps + step_idx * row_block
        slab_block = lax.dynamic_slice_in_dim(slab_cols, first_row, row_block, 0)
        tile_block = lax.dynamic_slice_in_dim(design, first_row, row_block, 0)
        is_live = position + step_idx * row_block < length
        live_block = jnp.where(is_live, slab_block, jnp.zeros((), slab_block.dtype))
        dims = (((0,), (0,)), ((), ()))
        normal_acc = running[0] + lax.dot_general(
            live_block, tile_block, dims, preferred_element_type=jnp.float32
        )
        gram_acc = running[1] + lax.dot_general(
            live_block, slab_block, dims, preferred_element_type=jnp.float32
        )
        return (normal_acc, gram_acc)

    partial_value, gram_part = lax.fori_loop(0, blocks_live, accumulate, (partial_value, gram_part))
    inverse_norm = 1.0 / math.sqrt(lax.axis_size("arc") * obs_dev)
    square_ids = lax.broadcasted_iota(jnp.int32, (slab_rows, slab_rows), 0)
    square_cols = lax.broadcasted_iota(jnp.int32, (slab_rows, slab_rows), 1)
    gram = lax.psum(gram_part, "arc") * inverse_norm
    gram = gram + jnp.where(square_ids == square_cols, kaula_prior[:, None], 0.0)
    gram_blocks = [gram[p * TILE : (p + 1) * TILE] for p in range(PANELS)]
    lowers = []
    couplings = {}
    for p in range(PANELS):
        lower_factor = jnp.linalg.cholesky(gram_blocks[p][:, p * TILE : (p + 1) * TILE])
        lowers.append(lower_factor)
        gram_blocks[p] = jax.scipy.linalg.solve_triangular(lower_factor, gram_blocks[p], lower=True)
        for q in range(p + 1, PANELS):
            upper_tile = gram_blocks[p][:, q * TILE : (q + 1) * TILE]
            couplings[p, q] = upper_tile
            gram_blocks[q] = gram_blocks[q] - jnp.dot(
                upper_tile.T, gram_blocks[p], precision=lax.Precision.HIGHEST
            )
    row_index = lax.broadcasted_iota(jnp.int32, (slab_rows, 1), 0)
    summed = lax.psum_scatter(partial_value, "arc", scatter_dimension=1, tiled=True) * inverse_norm
    width = ord_cols // lax.axis_size("arc")
    col_first = lax.axis_index("ord") * ord_cols + lax.axis_index("arc") * width
    global_col = col_first + lax.broadcasted_iota(jnp.int32, (1, width), 1)
    matrix = summed + jnp.where(row_index == global_col, kaula_prior[:, None], 0.0)
    share = apply_panels(matrix, lowers, couplings)
    factor = lax.all_to_all(share, "arc", split_axis=0, concat_axis=1, tiled=True)
    return factor


NB = 128
BAND = 5
GROUP = 64
LEVELS = 32760.0
PAD = 16
COLS = 256
VMEM_BYTES = 60 << 20
F32 = jnp.float32
BF16 = jnp.bfloat16


def params():
    return pltpu.CompilerParams(vmem_limit_bytes=VMEM_BYTES)


def cost(flops, moved):
    return pl.CostEstimate(flops=flops, bytes_accessed=moved, transcendentals=0)


def tree_sum(terms):
    while len(terms) > 1:
        pairs = [terms[i] + terms[i + 1] for i in range(0, len(terms) - 1, 2)]
        terms = pairs + ([terms[-1]] if len(terms) % 2 else [])
    return terms[0]


def diagonal_inverse(block):
    tiles = NB // 8
    sub = lax.broadcasted_iota(jnp.int32, (8, NB), 0)
    lane = lax.broadcasted_iota(jnp.int32, (8, NB), 1)
    rest = [block[8 * t : 8 * t + 8] for t in range(tiles)]
    inv = [jnp.where(sub + 8 * t == lane, 1.0, 0.0).astype(F32) for t in range(tiles)]

    def lanes(value, j):
        return jnp.broadcast_to(value[:, j : j + 1], (8, NB))

    def rows(value):
        return [jnp.broadcast_to(value[s : s + 1], (8, NB)) for s in range(8)]

    def combine(columns, row_values):
        return tree_sum([c * r for c, r in zip(columns, row_values)])

    for t in range(tiles):
        column = [lanes(rest[t], 8 * t + s) for s in range(8)]
        unit = [jnp.where(sub == s, 1.0, 0.0).astype(F32) for s in range(8)]
        whole = list(unit)
        pivots = jnp.ones((8, NB), F32)
        for s in range(8):
            pivot = jnp.broadcast_to(column[s][s : s + 1], (8, NB))
            recip = 1.0 / pivot
            pivots = jnp.where(sub == s, pivot, pivots)
            scaled = column[s] * recip
            below = jnp.where(sub > s, scaled, 0.0)
            others = jnp.where(sub == s, 1.0 - recip, scaled)
            for q in range(s + 1, 8):
                column[q] = column[q] - others * jnp.broadcast_to(column[q][s : s + 1], (8, NB))
            for q in range(s + 1):
                whole[q] = whole[q] - others * jnp.broadcast_to(whole[q][s : s + 1], (8, NB))
                unit[q] = unit[q] - below * jnp.broadcast_to(unit[q][s : s + 1], (8, NB))
        inv_rows = rows(inv[t])
        if t + 1 < tiles:
            solved = rows(combine(whole, rows(rest[t])))
            inv_solved = rows(combine(whole, inv_rows))
            for i in range(t + 1, tiles):
                columns = [lanes(rest[i], 8 * t + s) for s in range(8)]
                rest[i] = rest[i] - combine(columns, solved)
                inv[i] = inv[i] - combine(columns, inv_solved)
        inv[t] = combine(unit, inv_rows) * (1.0 / jnp.sqrt(pivots))
    return jnp.concatenate(inv, axis=0)


def exact_dot(a, b):
    return jnp.dot(a, b, precision=lax.Precision.HIGHEST)


def encode(value, group):
    height, width = value.shape
    grouped = value.reshape(height // group, group, width)
    top = jnp.max(jnp.abs(grouped), axis=1)
    index = jnp.ceil(jnp.log2(jnp.maximum(top, 1e-30)) * 8.0)
    factor = jnp.exp2(index * -0.125) * LEVELS
    code = jnp.round(grouped * factor[:, None, :]).astype(jnp.int32).astype(jnp.int16)
    return code.reshape(height, width), index


def decode(code, index, group):
    height, width = code.shape
    step = jnp.exp2(index * 0.125) * (1.0 / LEVELS)
    grouped = code.astype(jnp.int32).astype(F32).reshape(height // group, group, width)
    return (grouped * step[:, None, :]).reshape(height, width)


def levels(value, size):
    return value.astype(jnp.int32).astype(F32)[: size // GROUP]


def split(value):
    high = value.astype(BF16)
    return high, (value - high.astype(F32)).astype(BF16)


MESH = pl.DeviceIdType.MESH
WIDE = 512


def start_factor(gathered, prior_ref, work, scale):
    size = work.shape[0]
    blocks = size // NB
    sub = lax.broadcasted_iota(jnp.int32, (NB, NB), 0)
    lane = lax.broadcasted_iota(jnp.int32, (NB, NB), 1)
    eye = jnp.where(sub == lane, 1.0, 0.0).astype(F32)

    def band(i, d):
        parts = gathered[i // 4, i // 2 % 2, i % 2, :, :, d * NB : (d + 1) * NB]
        return parts.reshape(NB, NB)

    for i in range(blocks):
        here = slice(i * NB, (i + 1) * NB)
        for j in range(blocks):
            if j < i:
                value = jnp.zeros((NB, NB), F32)
            elif j - i < BAND:
                value = band(i, j - i) * scale
            else:
                value = band(j, i - j + blocks).T * scale
            if i == j:
                value = value + eye * prior_ref[i : i + 1, :]
            work[here, j * NB : (j + 1) * NB] = value


def factor_steps(first, last, work, upper, left):
    size = work.shape[0]
    blocks = size // NB
    sub = lax.broadcasted_iota(jnp.int32, (NB, NB), 0)
    lane = lax.broadcasted_iota(jnp.int32, (NB, NB), 1)
    eye = jnp.where(sub == lane, 1.0, 0.0).astype(F32)

    def step(k, carry):
        here = pl.ds(pl.multiple_of(k * NB, NB), NB)
        block = work[here, here]
        inverse = diagonal_inverse(block)
        work[here, here] = eye
        left[...] = exact_dot(inverse, work[here, :])
        column = lax.broadcasted_iota(jnp.int32, (NB, size), 1)
        upper[here, :] = jnp.where(column >= (k + 1) * NB, left[...], 0.0)
        upper[here, here] = exact_dot(inverse, block)
        work[here, :] = jnp.where(column < (k + 1) * NB, left[...], 0.0)

        def update(i, carry):
            there = pl.ds(pl.multiple_of(i * NB, NB), NB)
            work[there, here] = jnp.zeros((NB, NB), F32)
            work[there, :] -= exact_dot(left[:, there].T, left[...])
            return carry

        return lax.fori_loop(k + 1, blocks, update, carry)

    lax.fori_loop(first, last, step, 0)


def whole_kernel(
    scale,
    length_ref, design_ref, prior_ref, code_out, index_out, raw_ref,
    tiles, mask, other, band, first, sums, second, third, fourth, last, gathered,
    work, upper, left, away, across, upward, own, code, index,
    local_sem, tile_sem, raw_send, raw_recv, mask_send, mask_recv, swap_send, swap_recv,
    hop_send, hop_recv, gather_send, gather_recv, x_send, x_recv, z_send, z_recv,
    code_send, code_recv, index_send, index_recv,
):
    steps, ord_cols = design_ref.shape
    size = work.shape[0]
    blocks = size // NB
    arcs = code.shape[0]
    group = code.shape[1]
    rows = size // 2
    width = ord_cols // arcs
    me, order = lax.axis_index("arc"), lax.axis_index("ord")
    core, x, low, high = me % 2, me // 2 % 2, me // 4 % 2, me // 8
    peer = [
        (me + 1 - 2 * core, order),
        (me + 2 - 4 * x, order),
        (me + 4 - 8 * low, order),
        (me + 8 - 16 * high, order),
    ]
    opposite = (me, 1 - order)

    barrier = pltpu.get_barrier_semaphore()

    def greet(s, carry):
        device = (lax.rem(me + s, arcs), order)
        pl.semaphore_signal(barrier, inc=1, device_id=device, device_id_type=MESH)
        return carry

    lax.fori_loop(1, arcs, greet, 0)
    pl.semaphore_signal(barrier, inc=1, device_id=opposite, device_id_type=MESH)
    pl.semaphore_wait(barrier, arcs)

    def remote(source, target, send_sem, recv_sem, device):
        return pltpu.make_async_remote_copy(
            src_ref=source, dst_ref=target, send_sem=send_sem, recv_sem=recv_sem,
            device_id=device, device_id_type=MESH,
        )

    def place(k):
        z_high = high if k < 2 else 1 - high
        z_low = low if k % 2 == 0 else 1 - low
        return 2 * z_high + z_low

    raws = []
    for k in range(4):
        columns = pl.ds(pl.multiple_of(((1 - core) * 4 + place(k)) * 2 * width, width), 2 * width)
        raws.append(
            remote(design_ref.at[:, columns], raw_ref.at[k], raw_send.at[k], raw_recv.at[k], peer[0])
        )
    masks = [
        remote(mask.at[h], mask.at[h], mask_send.at[h], mask_recv.at[h], opposite) for h in range(2)
    ]
    swaps = [
        remote(mask.at[h], other.at[h], swap_send.at[h], swap_recv.at[h], peer[0]) for h in range(2)
    ]
    hops = [
        remote(band.at[:, :, :, 1 - core], first, hop_send.at[0], hop_recv.at[0], peer[0]),
        remote(sums.at[:, :, 1 - x], second, hop_send.at[1], hop_recv.at[1], peer[1]),
        remote(second.at[:, 1 - low], third, hop_send.at[2], hop_recv.at[2], peer[2]),
        remote(third.at[1 - high], fourth, hop_send.at[3], hop_recv.at[3], peer[3]),
        remote(fourth, last, hop_send.at[4], hop_recv.at[4], opposite),
    ]
    held = [
        (gathered.at[high, low, x, core], peer[1]),
        (gathered.at[high, low, :, core], peer[3]),
        (gathered.at[:, low, :, core], peer[2]),
        (gathered.at[:, :, :, core], peer[0]),
    ]
    gathers = [
        remote(part, part, gather_send.at[i], gather_recv.at[i], device)
        for i, (part, device) in enumerate(held)
    ]
    xs = [remote(away.at[n], across.at[n], x_send.at[n], x_recv.at[n], peer[1]) for n in range(8)]
    zs = [
        remote(
            away.at[4 * h + 3 - k], upward.at[3 * h + k - 1], z_send.at[3 * h + k - 1],
            z_recv.at[3 * h + k - 1], peer[3] if k == 2 else peer[2],
        )
        for h in range(2) for k in (1, 2, 3)
    ]

    stages = [(0, 3, 1), (0, 2, 1), (0, 1, 1), (0, 0, 1), (1, 3, 1), (1, 2, 1), (0, 3, 0), (1, 1, 1)]
    stages += [(1, 0, 1), (0, 2, 0), (0, 1, 0), (1, 3, 0), (1, 2, 0), (1, 1, 0), (0, 0, 0), (1, 0, 0)]

    def loads(n, t):
        _, k, flip = stages[n]
        block = x if flip == 0 else 1 - x
        mine = ((core * 4 + place(k)) * 2 + block) * width + t * WIDE
        theirs = block * width + t * WIDE
        return [
            pltpu.make_async_copy(
                design_ref.at[:, pl.ds(pl.multiple_of(mine, WIDE), WIDE)], tiles.at[t, 0], tile_sem.at[t, 0]
            ),
            pltpu.make_async_copy(
                raw_ref.at[k, :, pl.ds(pl.multiple_of(theirs, WIDE), WIDE)], tiles.at[t, 1], tile_sem.at[t, 1]
            ),
        ]

    def begin(n, t):
        if n < 4 and t == 0:
            raws[stages[n][1]].wait_recv()
        for load in loads(n, t):
            load.start()

    def stage(n, arrived, out, coded=True):
        h = stages[n][0]
        for t in range(width // WIDE):
            if t == 0:
                begin(n, 1)
            elif n + 1 < len(stages):
                begin(n + 1, 0)
            for load in loads(n, t):
                load.wait()

            def column(j, carry):
                part = pl.ds(pl.multiple_of(j * COLS, COLS), COLS)
                to = pl.ds(pl.multiple_of(t * WIDE + j * COLS, COLS), COLS)
                total = jnp.dot(mask[h], tiles[t, 0, :, part], preferred_element_type=F32)
                total = total + jnp.dot(other[h], tiles[t, 1, :, part], preferred_element_type=F32)
                for ref in arrived:
                    total = total + decode(ref[:rows, to], levels(ref[rows:, to], rows), GROUP)
                if coded:
                    value, level = encode(total, GROUP)
                    out[:rows, to] = value
                    level = jnp.concatenate([level, jnp.zeros((PAD - rows // GROUP, COLS), F32)], axis=0)
                    out[rows:, to] = level.astype(jnp.int32).astype(jnp.int16)
                else:
                    out[:, to] = total
                return carry

            lax.fori_loop(0, WIDE // COLS, column, 0)

    @pl.when(order == 0)
    def _():
        slab = [
            pltpu.make_async_copy(
                design_ref.at[:, pl.ds(c * WIDE, WIDE)], tiles.at[c, 0], local_sem.at[c]
            )
            for c in range(2)
        ]
        for load in slab:
            load.start()
        position = lax.broadcasted_iota(jnp.int32, (steps, NB), 0)
        per = blocks // 2
        for h in range(2):
            slab[h].wait()
            for i in range(per):
                piece = tiles[h, 0, :, i * NB : (i + 1) * NB].astype(F32)
                piece = jnp.where(position < length_ref[0], piece, 0.0)
                mask[h, i * NB : (i + 1) * NB, :] = piece.T.astype(BF16)
            masks[h].start()
            swaps[h].start()
            if h == 0:
                raws[3].start()
        for k in (2, 1, 0):
            raws[k].start()
        for i in range(blocks):
            lines = mask[i // per, i % per * NB : (i % per + 1) * NB, :]
            for d in range(BAND):
                j = (i + d) % blocks
                value = jnp.dot(
                    lines, tiles[j // per, 0, :, j % per * NB : (j % per + 1) * NB],
                    preferred_element_type=F32,
                )
                band[i // 4, i // 2 % 2, i % 2, :, :, d * NB : (d + 1) * NB] = value.reshape(
                    2, NB // 2, NB
                )
        hops[0].start()

    @pl.when(order == 1)
    def _():
        for k in (3, 2, 1, 0):
            raws[k].start()
        masks[0].wait_recv()
        swaps[0].start()

    def hop(step):
        @pl.when(order == 0)
        def _():
            hops[step].wait()
            if step == 0:
                sums[...] = band[:, :, :, core] + first[...]
            elif step == 1:
                second[...] = second[...] + sums[:, :, x]
            elif step == 2:
                third[...] = third[...] + second[:, low]
            else:
                fourth[...] = fourth[...] + third[high]
            hops[step + 1].start()

    def outgoing(n):
        h, k, _ = stages[n]
        stage(n, (), away.at[4 * h + 3 - k])

    def pump(m):
        xs[m].wait_send()
        if m + 2 < 8:
            xs[m + 2].start()

    def incoming(n):
        h, k, _ = stages[n]
        m = 4 * h + 3 - k
        xs[m].wait_recv()
        arrived = [across.at[m]]
        if k == 2:
            zs[3 * h + 2].wait_recv()
            arrived.append(upward.at[3 * h + 2])
        stage(n, arrived, away.at[m])
        zs[3 * h + k - 1].start()

    def steps_of(first, last):
        factor_steps(first, last, work, upper, left)

    begin(0, 0)
    hop(0)
    swaps[0].wait_recv()
    outgoing(0)
    xs[0].start()
    hop(1)
    outgoing(1)
    xs[1].start()
    hop(2)
    outgoing(2)
    hop(3)

    @pl.when(order == 0)
    def _():
        hops[4].wait_send()
        gathered[high, low, x, core] = fourth[...]

    @pl.when(order == 1)
    def _():
        masks[1].wait_recv()
        swaps[1].start()
        hops[4].wait_recv()
        gathered[high, low, x, core] = last[...]

    gathers[0].start()
    outgoing(3)
    gathers[0].wait()
    gathers[1].start()
    swaps[1].wait_recv()
    outgoing(4)
    outgoing(5)
    gathers[1].wait()
    gathers[2].start()
    pump(0)
    incoming(6)
    pump(1)
    outgoing(7)
    outgoing(8)
    gathers[2].wait()
    gathers[3].start()
    gathers[3].wait()
    start_factor(gathered, prior_ref, work, scale)
    steps_of(0, 1)
    pump(2)
    incoming(9)
    incoming(10)
    steps_of(1, 3)
    pump(3)
    steps_of(3, 4)
    pump(4)
    incoming(11)
    steps_of(4, 6)
    pump(5)
    incoming(12)
    steps_of(6, 8)
    pump(6)
    incoming(13)
    for h in range(2):
        stage(14 + h, (), own.at[h], coded=False)
    pump(7)
    for h in range(2):
        xs[4 * h + 3].wait_recv()
    for h in range(2):
        zs[3 * h].wait_recv()
        zs[3 * h + 1].wait_recv()

    use_upper = jnp.logical_and(order == 0, me == 0)
    chunk = 2 * NB

    def code_copy(half, s):
        to = lax.rem(me + s, arcs)
        columns = pl.ds(half * WIDE, WIDE)
        return remote(
            code.at[to, :, columns], code_out.at[me, :, columns],
            code_send.at[half, s - 1], code_recv.at[half, s - 1], (to, order),
        )

    def index_copy(s):
        to = lax.rem(me + s, arcs)
        return remote(
            index.at[to], index_out.at[me], index_send.at[s - 1], index_recv.at[s - 1], (to, order)
        )

    for half in range(2):
        def column(j, carry):
            to = pl.ds(pl.multiple_of(half * WIDE + j * COLS, COLS), COLS)
            highs, lows = [], []
            for h in range(2):
                value = own[h, :, to]
                for ref in (across.at[4 * h + 3], upward.at[3 * h], upward.at[3 * h + 1]):
                    value = value + decode(ref[:rows, to], levels(ref[rows:, to], rows), GROUP)
                top, rest = split(value * scale)
                highs.append(top)
                lows.append(rest)
            top, rest = jnp.concatenate(highs, axis=0), jnp.concatenate(lows, axis=0)
            for i in range(size // chunk):
                here = slice(i * chunk, (i + 1) * chunk)
                depth = (i + 1) * chunk
                a_top, a_rest = split(work[here, :depth])
                value = jnp.dot(a_top, top[:depth], preferred_element_type=F32)
                value = value + jnp.dot(a_top, rest[:depth], preferred_element_type=F32)
                value = value + jnp.dot(a_rest, top[:depth], preferred_element_type=F32)
                value = jnp.where(use_upper, upper[here, to], value)
                codes, level = encode(value, group)
                for g in range(chunk // group):
                    code[i * (chunk // group) + g, :, to] = codes[g * group : (g + 1) * group]
                    index[i * (chunk // group) + g, :, to] = level[g : g + 1]
            return carry

        lax.fori_loop(0, WIDE // COLS, column, 0)

        def launch(s, carry):
            code_copy(half, s).start()
            return carry

        lax.fori_loop(1, arcs, launch, 0)

    def launch_index(s, carry):
        index_copy(s).start()
        return carry

    lax.fori_loop(1, arcs, launch_index, 0)
    keeps = [
        pltpu.make_async_copy(code.at[me], code_out.at[me], local_sem.at[0]),
        pltpu.make_async_copy(index.at[me], index_out.at[me], local_sem.at[1]),
    ]
    for keep in keeps:
        keep.start()

    @pl.when(order == 0)
    def _():
        for h in range(2):
            masks[h].wait_send()
    for h in range(2):
        swaps[h].wait_send()
    for raw in raws:
        raw.wait_send()
    for z in zs:
        z.wait_send()

    def finish(s, carry):
        for half in range(2):
            code_copy(half, s).wait()
        index_copy(s).wait()
        return carry

    lax.fori_loop(1, arcs, finish, 0)
    for keep in keeps:
        keep.wait()


def whole(design, arc_lengths, prior, size, arcs, scale):
    steps, ord_cols = design.shape
    width = ord_cols // arcs
    group = NB // 2
    span = BAND * NB
    rows = size // 2
    anywhere = pl.BlockSpec(memory_space=pl.ANY)
    sems = pltpu.SemaphoreType.DMA
    vmem = pltpu.VMEM
    int16 = jnp.int16
    code, index, _ = pl.pallas_call(
        functools.partial(whole_kernel, scale),
        out_shape=(
            jax.ShapeDtypeStruct((arcs, size // arcs, width), int16),
            jax.ShapeDtypeStruct((arcs, 1, width), F32),
            jax.ShapeDtypeStruct((4, steps, 2 * width), BF16),
        ),
        in_specs=[pl.BlockSpec(memory_space=pltpu.SMEM), anywhere, pl.BlockSpec(memory_space=vmem)],
        out_specs=(anywhere, anywhere, anywhere),
        scratch_shapes=[
            vmem((2, 2, steps, WIDE), BF16),
            vmem((2, rows, steps), BF16),
            vmem((2, rows, steps), BF16),
            vmem((2, 2, 2, 2, group, span), F32),
            vmem((2, 2, 2, group, span), F32),
            vmem((2, 2, 2, group, span), F32),
            vmem((2, 2, group, span), F32),
            vmem((2, group, span), F32),
            vmem((group, span), F32),
            vmem((group, span), F32),
            vmem((2, 2, 2, 2, group, span), F32),
            vmem((size, size), F32),
            vmem((size, size), F32),
            vmem((NB, size), F32),
            vmem((8, rows + PAD, width), int16),
            vmem((8, rows + PAD, width), int16),
            vmem((6, rows + PAD, width), int16),
            vmem((2, rows, width), F32),
            vmem((arcs, size // arcs, width), int16),
            vmem((arcs, 1, width), F32),
            sems((2,)), sems((2, 2)), sems((4,)), sems((4,)), sems((2,)), sems((2,)), sems((2,)), sems((2,)),
            sems((5,)), sems((5,)), sems((4,)), sems((4,)), sems((8,)), sems((8,)), sems((6,)), sems((6,)),
            sems((2, arcs - 1)), sems((2, arcs - 1)), sems((arcs - 1,)), sems((arcs - 1,)),
        ],
        compiler_params=pltpu.CompilerParams(
            vmem_limit_bytes=VMEM_BYTES, collective_id=0, has_side_effects=True
        ),
        cost_estimate=cost(300_000_000_000, 100 << 20),
    )(arc_lengths, design, prior.reshape(size // NB, NB))
    return code, index


def decode_kernel(code_ref, index_ref, out_ref):
    chips, _, group, width = code_ref.shape
    for c in range(chips):
        step = jnp.exp2(index_ref[c, 0] * 0.125) * (1.0 / LEVELS)
        out_ref[:, c * width : (c + 1) * width] = code_ref[c, 0].astype(jnp.int32).astype(F32) * step


def decode_rows(code, index):
    arcs, group, width = code.shape
    half, per = arcs // 2, 4
    place = lambda j: (j % (half // per), j // (half // per), 0, 0)
    return pl.pallas_call(
        decode_kernel,
        out_shape=jax.ShapeDtypeStruct((group, arcs * width), F32),
        grid=(arcs // per,),
        in_specs=[
            pl.BlockSpec((per, 1, group, width), place),
            pl.BlockSpec((per, 1, 1, width), place),
        ],
        out_specs=pl.BlockSpec((group, per * width), lambda j: (0, j)),
        compiler_params=params(),
        cost_estimate=cost(2 * arcs * group * width, 6 << 20),
    )(code.reshape(half, 2, group, width), index.reshape(half, 2, 1, width))


def on_device_paired(design, arc_lengths, kaula_prior):
    arcs = lax.axis_size("arc")
    inverse_norm = 1.0 / math.sqrt(arcs * design.shape[0])
    code, index = whole(design, arc_lengths, kaula_prior, TILE * PANELS, arcs, inverse_norm)
    return decode_rows(code, index)


def solution(mesh):
    in_specs = (P("arc", "ord"), P("arc"), P())
    out_specs = P("arc", "ord")
    paired = mesh.shape["arc"] == 16 and mesh.shape["ord"] == 2
    return jax.shard_map(
        on_device_paired if paired else on_device,
        mesh=mesh, in_specs=in_specs, out_specs=out_specs, check_vma=False
    )
```
